128 devices in a mesh: ray: 8 (over z, core), cell: 16 (over x, y).
Axes of the slice: x: 4, y: 4, z: 4, core: 2. Of those that a mesh axis runs over, the one named last changes fastest.
Arguments:
- right_side: float32 [8, 16384], P(None, 'ray'), may hold values from -6 to 6
- tiles: bfloat16 [64, 64, 256, 256], P('ray', 'cell'), may hold values from -0.375 to 0.375
- pattern: int32 [64, 64], P('ray', 'cell'), may hold values from 0 to 31, as said below
- counts: int32 [64, 16], P('ray', 'cell'), may hold values from 1 to 4, as said below
Outputs:
- solution: float32 [8, 131072], P(None, 'cell')
- misfit: float32 [8], replicated
The draws below stay inside these ranges and needn't reach their ends.
Inputs may be any that keep to these rules, and one draw needn't show every extreme that they name: `pattern`: each entry indexes a block within the slot's group of 32 cell blocks; a bundle may name a block more than once. Ragged counts; some bundle has all 4 slots live in some group, and some has one.
All inputs are finite; a program needn't handle non-finite values.
Results may differ from the reference program's by a relative error of at most 0.0014.
Values may be sent and summed in bfloat16 or wider, within the bound.
No kernel may reach another device: no remote copies, remote signals or barrier semaphores. Data moves between devices by JAX's collectives and lax.ppermute only.
A program may use at most 64 MiB of HBM per device.

```python
import jax
import jax.numpy as jnp
from jax import lax

RB = 256
CB = 256
NRHS = 8
BLK_DEV = 32
KDEV = 4
ITERS = 4
SHARDS = 16
BUNDLES = 64
BLOCKS = 512
SLOTS = 64
ROWS = 16384
CELLS = 131072


def draw_pattern(key, part):
    values = jax.random.randint(jax.random.fold_in(key, 11), (BUNDLES, SLOTS), 0, BLK_DEV)
    values = values.at[0, 0].set(0).at[0, 1].set(BLK_DEV - 1)
    return values.astype(jnp.int32)


def draw_counts(key, part):
    values = jax.random.randint(jax.random.fold_in(key, 23), (BUNDLES, SHARDS), 1, KDEV + 1)
    values = values.at[0, 0].set(KDEV).at[1, 0].set(1)
    return values.astype(jnp.int32)


def shard_levels(own_key, dims, split, least, top_value):
    loudness, own = 1.0, jax.random.fold_in(own_key, 6)
    for axis_at, blocks in split:
        steps = jnp.exp(jax.random.uniform(jax.random.fold_in(own, axis_at), (blocks,), jnp.float32, least / len(split), top_value / len(split)))
        loudness = loudness * jnp.repeat(steps, dims[axis_at] // blocks).reshape([-1 if axis == axis_at else 1 for axis in range(len(dims))])
    return loudness


def noise(key, shape, scale, reach, pieces=(), kind=jnp.bfloat16):
    values = jax.random.normal(key, shape, jnp.float32) * scale
    if len(pieces) > 0:
        values = shard_levels(key, shape, pieces, -0.22, 0.18) * values
    return jnp.clip(values, min=-reach, max=reach).astype(kind)


def setup_inputs(seed: int = 0) -> dict:
    streams_of = jax.random.split(jax.random.key(seed), 5)
    right_side = noise(streams_of[0], (NRHS, ROWS), 1.0, 6.0, ((1, 8),), jnp.float32)
    tiles = noise(streams_of[1], (BUNDLES, SLOTS, RB, CB), CB ** -0.5, 0.375, ((0, 8), (1, 16)))
    pattern = draw_pattern(jax.random.fold_in(streams_of[4], 71), 0)
    counts = draw_counts(jax.random.fold_in(streams_of[4], 71), 0)
    return dict(right_side=right_side, tiles=tiles, pattern=pattern, counts=counts)


def slot_info(pattern_row, count_row):
    slot = jnp.arange(SLOTS, dtype=jnp.int32)
    group = slot // KDEV
    live = slot % KDEV < count_row[group]
    target = (group * BLK_DEV + pattern_row).astype(jnp.int32)
    return (live, target)

def forward(tiles, pattern, counts, vector):
    nrhs = vector.shape[0]
    vblocks = vector.astype(jnp.bfloat16).reshape(nrhs, BLOCKS, CB)

    def one(args):
        tile, pattern_row, count_row = args
        live, target = slot_info(pattern_row, count_row)
        picked = vblocks[:, target].astype(jnp.float32) * live[None, :, None].astype(jnp.float32)
        return jnp.einsum('src,nsc->nr', tile.astype(jnp.float32), picked)
    out = lax.map(one, (tiles, pattern, counts))
    return jnp.transpose(out, (1, 0, 2)).reshape(nrhs, ROWS)

def adjoint(tiles, pattern, counts, vector):
    nrhs = vector.shape[0]
    ublocks = jnp.transpose(vector.astype(jnp.bfloat16).reshape(nrhs, BUNDLES, RB), (1, 0, 2))

    def one(carry, args):
        tile, pattern_row, count_row, rows = args
        live, target = slot_info(pattern_row, count_row)
        per = jnp.einsum('src,nr->snc', tile.astype(jnp.float32), rows.astype(jnp.float32))
        per = per * live[:, None, None].astype(jnp.float32)
        return (carry.at[:, target].add(jnp.transpose(per, (1, 0, 2))), None)
    start = jnp.zeros((nrhs, BLOCKS, CB), jnp.float32)
    total, _ = lax.scan(one, start, (tiles, pattern, counts, ublocks))
    return total.reshape(nrhs, CELLS)

def norm_of(vector):
    return jnp.sqrt(lax.optimization_barrier(jnp.sum(vector * vector, axis=1)) + 1e-06)

def reference(right_side, tiles, pattern, counts):
    beta = norm_of(right_side)
    u = right_side / beta[:, None]
    v = adjoint(tiles, pattern, counts, u)
    alpha = norm_of(v)
    v = v / alpha[:, None]
    w = v
    x = jnp.zeros_like(v)
    phibar = beta
    rhobar = alpha
    for step in range(ITERS):
        u = forward(tiles, pattern, counts, v) - alpha[:, None] * u
        beta = norm_of(u)
        u = u / beta[:, None]
        v = adjoint(tiles, pattern, counts, u) - beta[:, None] * v
        alpha = norm_of(v)
        v = v / alpha[:, None]
        rho = jnp.sqrt(rhobar * rhobar + beta * beta)
        cosine = rhobar / rho
        sine = beta / rho
        theta = sine * alpha
        rhobar = -cosine * alpha
        phi = cosine * phibar
        phibar = sine * phibar
        x = x + (phi / rho)[:, None] * w
        w = v - (theta / rho)[:, None] * w
    return (x, phibar)
```

```python
import functools

import jax
import jax.numpy as jnp
from jax import lax
from jax.experimental import pallas as pl
from jax.experimental.pallas import tpu as pltpu
from jax.sharding import Mesh, PartitionSpec as P

BLK_DEV = 32
ITERS = 4
EPS = 1e-06
F32 = jnp.float32
BF16 = jnp.bfloat16

VMEM = pl.BlockSpec(memory_space=pltpu.VMEM)
SMEM = pl.BlockSpec(memory_space=pltpu.SMEM)


def lane_sum(x):
    return jnp.sum(x, axis=1, keepdims=True)


def fold_sq(x, width):
    total = None
    for at in range(0, x.shape[1], width):
        piece = x[:, at : at + width]
        total = piece * piece if total is None else total + piece * piece
    return total


def wide(x):
    return jnp.broadcast_to(x, (x.shape[0], 128))


def scatter_products(u, place_ref, tiles_ref, keep_ref, send_ref, acc_ref):
    bundles, slots, rays, cells = tiles_ref.shape
    half = keep_ref.shape[1]
    acc_ref[...] = jnp.zeros_like(acc_ref)
    low = u.astype(BF16)
    for b in range(bundles):
        rows = low[:, b * rays : (b + 1) * rays]
        for s in range(slots):
            part = jnp.dot(rows, tiles_ref[b, s], preferred_element_type=F32)
            at = pl.multiple_of(place_ref[b * slots + s] * cells, cells)
            acc_ref[:, pl.ds(at, cells)] += part
    squares = fold_sq(u, cells)
    for out_ref, at in ((keep_ref, 0), (send_ref, half)):
        out_ref[:, : half - cells] = acc_ref[:, at : at + half - cells]
        out_ref[:, half - cells :] = squares


def first_adjoint(place_ref, right_ref, tiles_ref, keep_ref, send_ref, acc_ref):
    scatter_products(right_ref[...], place_ref, tiles_ref, keep_ref, send_ref, acc_ref)


def ray_vector(own_ref, left_ref, right_ref, far_ref, prev_ref, beta_ref):
    total = (own_ref[...] + far_ref[...]) + (left_ref[...] + right_ref[...])
    rows = prev_ref.shape[1]
    alpha = jnp.sqrt(lane_sum(total[:, rows:]) + EPS)
    u = total[:, :rows] / alpha - (alpha / beta_ref[:, :1]) * prev_ref[...]
    return u, alpha


def next_adjoint(
    place_ref, own_ref, left_ref, right_ref, far_ref, prev_ref, beta_ref, tiles_ref,
    keep_ref, send_ref, u_ref, alpha_ref, acc_ref,
):
    u, alpha = ray_vector(own_ref, left_ref, right_ref, far_ref, prev_ref, beta_ref)
    u_ref[...] = u
    alpha_ref[...] = wide(alpha)
    scatter_products(u, place_ref, tiles_ref, keep_ref, send_ref, acc_ref)


def last_norm(
    own_ref, left_ref, right_ref, far_ref, prev_ref, beta_ref, out_ref, alpha_ref
):
    u, alpha = ray_vector(own_ref, left_ref, right_ref, far_ref, prev_ref, beta_ref)
    alpha_ref[...] = wide(alpha)
    out_ref[...] = fold_sq(u, 128)


def cell_vector(
    first, own_ref, left_ref, right_ref, far_ref, prev_ref, alpha_ref, v_ref, beta_ref
):
    total = (own_ref[...] + far_ref[...]) + (left_ref[...] + right_ref[...])
    width = v_ref.shape[1]
    beta = jnp.sqrt(lane_sum(total[:, width:]) + EPS)
    v = total[:, :width] / beta
    if not first:
        v = v - (beta / alpha_ref[:, :1]) * prev_ref[...]
    v_ref[...] = v
    beta_ref[...] = wide(beta)


def forward(place_ref, own_ref, other_ref, tiles_ref, out_ref, low_ref):
    bundles, slots, rays, cells = tiles_ref.shape
    width = own_ref.shape[1]
    own, other = own_ref[...], other_ref[...]
    low_ref[:, :width] = own.astype(BF16)
    low_ref[:, width : 2 * width] = other.astype(BF16)
    low_ref[:, 2 * width :] = jnp.zeros((own.shape[0], cells), BF16)
    base = bundles * slots
    for b in range(bundles):
        acc = None
        for s in range(slots):
            at = pl.multiple_of(place_ref[base + b * slots + s] * cells, cells)
            part = lax.dot_general(
                low_ref[:, pl.ds(at, cells)], tiles_ref[b, s],
                (((1,), (1,)), ((), ())), preferred_element_type=F32,
            )
            acc = part if acc is None else acc + part
        out_ref[:, b * rays : (b + 1) * rays] = acc
    out_ref[:, bundles * rays :] = fold_sq(own, cells) + fold_sq(other, cells)


def finish(place_ref, own_ref, left_ref, right_ref, far_ref, *rest):
    count = ITERS
    own_refs, other_refs = rest[:count], rest[count : 2 * count]
    alpha_refs, beta_refs = rest[2 * count : 3 * count], rest[3 * count : 4 * count]
    x_ref, misfit_ref = rest[4 * count :]
    width = own_refs[0].shape[1]
    total = (own_ref[...] + far_ref[...]) + (left_ref[...] + right_ref[...])
    last_beta = jnp.sqrt(lane_sum(total) + EPS)
    alphas = [ref[:, :1] for ref in alpha_refs]
    betas = [ref[:, :1] for ref in beta_refs] + [last_beta]
    phibar, rhobar = betas[0], alphas[0]
    steps, turns = [], []
    for k in range(count):
        beta = betas[k + 1]
        rho = jnp.sqrt(rhobar * rhobar + beta * beta)
        cosine, sine = rhobar / rho, beta / rho
        phi = cosine * phibar
        phibar = sine * phibar
        steps.append(phi / rho)
        if k + 1 < count:
            theta = sine * alphas[k + 1]
            rhobar = -cosine * alphas[k + 1]
            turns.append(theta / rho)
    core = place_ref[place_ref.shape[0] - 1]
    for refs, half in ((own_refs, core), (other_refs, 1 - core)):
        w = refs[0][...] / alphas[0]
        x = steps[0] * w
        for k in range(1, count):
            w = refs[k][...] / alphas[k] - turns[k - 1] * w
            x = x + steps[k] * w
        x_ref[:, pl.ds(pl.multiple_of(half * width, width), width)] = x
    misfit_ref[...] = wide(phibar)


def call(body, outs, specs, args, scratch=()):
    return pl.pallas_call(
        body,
        out_shape=outs,
        in_specs=specs,
        out_specs=[VMEM] * len(outs),
        scratch_shapes=list(scratch),
        compiler_params=pltpu.CompilerParams(vmem_limit_bytes=40 << 20),
    )(*args)


def local(right_side, tiles, pattern, counts):
    nrhs, rows = right_side.shape
    bundles, slots, rays, cells = tiles.shape
    blocks = BLK_DEV // 2
    half = blocks * cells
    core = lax.axis_index("core")
    live = lax.broadcasted_iota(jnp.int32, pattern.shape, 1) < counts
    mine = pattern // blocks == core
    within = pattern % blocks
    put = jnp.where(live, jnp.where(mine, within, blocks + 1 + within), blocks)
    get = jnp.where(live, jnp.where(mine, within, blocks + within), BLK_DEV)
    place = jnp.concatenate([put.reshape(-1), get.reshape(-1), core.astype(jnp.int32).reshape(1)])

    def shape(columns, dtype=F32):
        return jax.ShapeDtypeStruct((nrhs, columns), dtype)

    def spread(value, axis):
        n = lax.axis_size(axis)
        moved = [
            lax.ppermute(value, axis, [(i, (i + by) % n) for i in range(n)]) for by in (1, 3, 2)
        ]
        return [value] + moved

    def swap(value):
        return lax.ppermute(value, "core", [(0, 1), (1, 0)])

    def over_cell(partial):
        own, left, right, far = spread(partial, "x")
        return spread((own + far) + (left + right), "y")

    halves = [shape(half + cells)] * 2
    store = [pltpu.VMEM((nrhs, 2 * (half + cells)), F32)]
    keep, send = call(
        first_adjoint, halves, [SMEM, VMEM, VMEM], (place, right_side, tiles), store
    )
    u = right_side
    owns, others, alphas, betas = [], [], [], []
    for step in range(ITERS):
        prev = (owns[-1], alphas[-1]) if step else (right_side, right_side)
        v, beta = call(
            functools.partial(cell_vector, step == 0), [shape(half), shape(128)], [VMEM] * 6,
            (*spread(keep + swap(send), "z"), *prev),
        )
        other = swap(v)
        owns.append(v)
        others.append(other)
        betas.append(beta)
        products, = call(
            forward, [shape(rows + cells)], [SMEM] + [VMEM] * 3, (place, v, other, tiles),
            [pltpu.VMEM((nrhs, 2 * half + cells), BF16)],
        )
        rows_in = over_cell(products)
        if step + 1 < ITERS:
            keep, send, u, alpha = call(
                next_adjoint, halves + [shape(rows), shape(128)], [SMEM] + [VMEM] * 7,
                (place, *rows_in, u, beta, tiles), store,
            )
        else:
            squares, alpha = call(
                last_norm, [shape(128), shape(128)], [VMEM] * 6, (*rows_in, u, beta)
            )
        alphas.append(alpha)
    x, misfit = call(
        finish, [shape(2 * half), shape(128)], [SMEM] + [VMEM] * (4 + 4 * ITERS),
        (place, *spread(squares + swap(squares), "z"), *owns, *others, *alphas, *betas),
    )
    return x, misfit[:, 0]


def solution(mesh):
    parts = Mesh(mesh.devices.reshape(4, 2, 4, 4), ("z", "core", "x", "y"))
    ray, cell = ("z", "core"), ("x", "y")
    in_specs = (P(None, ray), P(ray, cell, None, None), P(ray, cell), P(ray, cell))
    out_specs = (P(None, cell), P())
    return jax.shard_map(local, mesh=parts, in_specs=in_specs, out_specs=out_specs, check_vma=False)
```

```python
import functools

import jax
import jax.numpy as jnp
from jax import lax
from jax.experimental import pallas as pl
from jax.experimental.pallas import tpu as pltpu
from jax.sharding import Mesh, PartitionSpec as P

BLK_DEV = 32
ITERS = 4
EPS = 1e-06
F32 = jnp.float32
BF16 = jnp.bfloat16

VMEM = pl.BlockSpec(memory_space=pltpu.VMEM)
SMEM = pl.BlockSpec(memory_space=pltpu.SMEM)
HBM = pl.BlockSpec(memory_space=pltpu.HBM)


def lane_sum(x):
    return jnp.sum(x, axis=1, keepdims=True)


def fold_sq(x, width):
    total = None
    for at in range(0, x.shape[1], width):
        piece = x[:, at : at + width]
        total = piece * piece if total is None else total + piece * piece
    return total


def wide(x):
    return jnp.broadcast_to(x, (x.shape[0], 128))


def scatter_products(u, place_ref, tiles_ref, keep_ref, send_ref, acc_ref, copies=None):
    bundles, slots, rays, cells = tiles_ref.shape
    half = keep_ref.shape[1]
    acc_ref[...] = jnp.zeros_like(acc_ref)
    low = u.astype(BF16)
    for b in range(bundles):
        if copies:
            copies[b].wait()
        rows = low[:, b * rays : (b + 1) * rays]
        for s in range(slots):
            part = jnp.dot(rows, tiles_ref[b, s], preferred_element_type=F32)
            at = pl.multiple_of(place_ref[b * slots + s] * cells, cells)
            acc_ref[:, pl.ds(at, cells)] += part
    squares = fold_sq(u, cells)
    for out_ref, at in ((keep_ref, 0), (send_ref, half)):
        out_ref[:, : half - cells] = acc_ref[:, at : at + half - cells]
        out_ref[:, half - cells :] = squares


def first_adjoint(
    place_ref, right_ref, source_ref, keep_ref, send_ref, tiles_ref, acc_ref, sem
):
    copies = [
        pltpu.make_async_copy(source_ref.at[b], tiles_ref.at[b], sem.at[b])
        for b in range(source_ref.shape[0])
    ]
    for copy in copies:
        copy.start()
    scatter_products(right_ref[...], place_ref, tiles_ref, keep_ref, send_ref, acc_ref, copies)


def ray_vector(own_ref, left_ref, right_ref, far_ref, prev_ref, beta_ref):
    total = (own_ref[...] + far_ref[...]) + (left_ref[...] + right_ref[...])
    rows = prev_ref.shape[1]
    alpha = jnp.sqrt(lane_sum(total[:, rows:]) + EPS)
    u = total[:, :rows] / alpha - (alpha / beta_ref[:, :1]) * prev_ref[...]
    return u, alpha


def next_adjoint(
    place_ref, own_ref, left_ref, right_ref, far_ref, prev_ref, beta_ref, tiles_ref,
    keep_ref, send_ref, u_ref, alpha_ref, acc_ref,
):
    u, alpha = ray_vector(own_ref, left_ref, right_ref, far_ref, prev_ref, beta_ref)
    u_ref[...] = u
    alpha_ref[...] = wide(alpha)
    scatter_products(u, place_ref, tiles_ref, keep_ref, send_ref, acc_ref)


def last_norm(
    own_ref, left_ref, right_ref, far_ref, prev_ref, beta_ref, out_ref, alpha_ref
):
    u, alpha = ray_vector(own_ref, left_ref, right_ref, far_ref, prev_ref, beta_ref)
    alpha_ref[...] = wide(alpha)
    out_ref[...] = fold_sq(u, 128)


def cell_vector(
    first, own_ref, left_ref, right_ref, far_ref, prev_ref, alpha_ref, v_ref, beta_ref
):
    total = (own_ref[...] + far_ref[...]) + (left_ref[...] + right_ref[...])
    width = v_ref.shape[1]
    beta = jnp.sqrt(lane_sum(total[:, width:]) + EPS)
    v = total[:, :width] / beta
    if not first:
        v = v - (beta / alpha_ref[:, :1]) * prev_ref[...]
    v_ref[...] = v
    beta_ref[...] = wide(beta)


def forward(place_ref, own_ref, other_ref, tiles_ref, out_ref, low_ref):
    bundles, slots, rays, cells = tiles_ref.shape
    width = own_ref.shape[1]
    own, other = own_ref[...], other_ref[...]
    low_ref[:, :width] = own.astype(BF16)
    low_ref[:, width : 2 * width] = other.astype(BF16)
    low_ref[:, 2 * width :] = jnp.zeros((own.shape[0], cells), BF16)
    base = bundles * slots
    for b in range(bundles):
        acc = None
        for s in range(slots):
            at = pl.multiple_of(place_ref[base + b * slots + s] * cells, cells)
            part = lax.dot_general(
                low_ref[:, pl.ds(at, cells)], tiles_ref[b, s],
                (((1,), (1,)), ((), ())), preferred_element_type=F32,
            )
            acc = part if acc is None else acc + part
        out_ref[:, b * rays : (b + 1) * rays] = acc
    out_ref[:, bundles * rays :] = fold_sq(own, cells) + fold_sq(other, cells)


def finish(place_ref, own_ref, left_ref, right_ref, far_ref, *rest):
    count = ITERS
    own_refs, other_refs = rest[:count], rest[count : 2 * count]
    alpha_refs, beta_refs = rest[2 * count : 3 * count], rest[3 * count : 4 * count]
    x_ref, misfit_ref = rest[4 * count :]
    width = own_refs[0].shape[1]
    total = (own_ref[...] + far_ref[...]) + (left_ref[...] + right_ref[...])
    last_beta = jnp.sqrt(lane_sum(total) + EPS)
    alphas = [ref[:, :1] for ref in alpha_refs]
    betas = [ref[:, :1] for ref in beta_refs] + [last_beta]
    phibar, rhobar = betas[0], alphas[0]
    steps, turns = [], []
    for k in range(count):
        beta = betas[k + 1]
        rho = jnp.sqrt(rhobar * rhobar + beta * beta)
        cosine, sine = rhobar / rho, beta / rho
        phi = cosine * phibar
        phibar = sine * phibar
        steps.append(phi / rho)
        if k + 1 < count:
            theta = sine * alphas[k + 1]
            rhobar = -cosine * alphas[k + 1]
            turns.append(theta / rho)
    core = place_ref[place_ref.shape[0] - 1]
    for refs, half in ((own_refs, core), (other_refs, 1 - core)):
        w = refs[0][...] / alphas[0]
        x = steps[0] * w
        for k in range(1, count):
            w = refs[k][...] / alphas[k] - turns[k - 1] * w
            x = x + steps[k] * w
        x_ref[:, pl.ds(pl.multiple_of(half * width, width), width)] = x
    misfit_ref[...] = wide(phibar)


def call(body, outs, specs, args, scratch=()):
    return pl.pallas_call(
        body,
        out_shape=outs,
        in_specs=specs,
        out_specs=[VMEM] * len(outs),
        scratch_shapes=list(scratch),
        compiler_params=pltpu.CompilerParams(vmem_limit_bytes=12 << 20),
    )(*args)


def local(right_side, tiles, pattern, counts):
    nrhs, rows = right_side.shape
    bundles, slots, rays, cells = tiles.shape
    blocks = BLK_DEV // 2
    half = blocks * cells
    core = lax.axis_index("core")
    live = lax.broadcasted_iota(jnp.int32, pattern.shape, 1) < counts
    mine = pattern // blocks == core
    within = pattern % blocks
    put = jnp.where(live, jnp.where(mine, within, blocks + 1 + within), blocks)
    get = jnp.where(live, jnp.where(mine, within, blocks + within), BLK_DEV)
    place = jnp.concatenate([put.reshape(-1), get.reshape(-1), core.astype(jnp.int32).reshape(1)])

    def shape(columns, dtype=F32):
        return jax.ShapeDtypeStruct((nrhs, columns), dtype)

    def spread(value, axis):
        n = lax.axis_size(axis)
        moved = [
            lax.ppermute(value, axis, [(i, i ^ by) for i in range(n)]) for by in (1, 3, 2)
        ]
        return [value] + moved

    def swap(value):
        return lax.ppermute(value, "core", [(0, 1), (1, 0)])

    def over_cell(partial):
        own, left, right, far = spread(partial, "x")
        return spread((own + far) + (left + right), "y")

    halves = [shape(half + cells)] * 2
    store = [pltpu.VMEM((nrhs, 2 * (half + cells)), F32)]
    keep, send, tiles = call(
        first_adjoint, halves + [jax.ShapeDtypeStruct(tiles.shape, tiles.dtype)],
        [SMEM, VMEM, HBM], (place, right_side, tiles),
        store + [pltpu.SemaphoreType.DMA((bundles,))],
    )
    u = right_side
    owns, others, alphas, betas = [], [], [], []
    for step in range(ITERS):
        prev = (owns[-1], alphas[-1]) if step else (right_side, right_side)
        v, beta = call(
            functools.partial(cell_vector, step == 0), [shape(half), shape(128)], [VMEM] * 6,
            (*spread(keep + swap(send), "z"), *prev),
        )
        other = swap(v)
        owns.append(v)
        others.append(other)
        betas.append(beta)
        products, = call(
            forward, [shape(rows + cells)], [SMEM] + [VMEM] * 3, (place, v, other, tiles),
            [pltpu.VMEM((nrhs, 2 * half + cells), BF16)],
        )
        rows_in = over_cell(products)
        if step + 1 < ITERS:
            keep, send, u, alpha = call(
                next_adjoint, halves + [shape(rows), shape(128)], [SMEM] + [VMEM] * 7,
                (place, *rows_in, u, beta, tiles), store,
            )
        else:
            squares, alpha = call(
                last_norm, [shape(128), shape(128)], [VMEM] * 6, (*rows_in, u, beta)
            )
        alphas.append(alpha)
    x, misfit = call(
        finish, [shape(2 * half), shape(128)], [SMEM] + [VMEM] * (4 + 4 * ITERS),
        (place, *spread(squares + swap(squares), "z"), *owns, *others, *alphas, *betas),
    )
    return x, misfit[:, 0]


def solution(mesh):
    parts = Mesh(mesh.devices.reshape(4, 2, 4, 4), ("z", "core", "x", "y"))
    ray, cell = ("z", "core"), ("x", "y")
    in_specs = (P(None, ray), P(ray, cell, None, None), P(ray, cell), P(ray, cell))
    out_specs = (P(None, cell), P())
    return jax.shard_map(local, mesh=parts, in_specs=in_specs, out_specs=out_specs, check_vma=False)
```

```python
import functools

import jax
import jax.numpy as jnp
from jax import lax
from jax.experimental import pallas as pl
from jax.experimental.pallas import tpu as pltpu
from jax.sharding import Mesh, PartitionSpec as P

BLK_DEV = 32
ITERS = 4
EPS = 1e-06
TINY = 1e-30
DIGITS = 8192.0
CODES = 32000.0
F32 = jnp.float32
BF16 = jnp.bfloat16

VMEM = pl.BlockSpec(memory_space=pltpu.VMEM)
SMEM = pl.BlockSpec(memory_space=pltpu.SMEM)
HBM = pl.BlockSpec(memory_space=pltpu.HBM)


def lane_sum(x):
    return jnp.sum(x, axis=1, keepdims=True)


def fold_sq(x, width):
    total = None
    for at in range(0, x.shape[1], width):
        piece = x[:, at : at + width]
        total = piece * piece if total is None else total + piece * piece
    return total


def wide(x):
    return jnp.broadcast_to(x, (x.shape[0], 128))


def scatter_products(u, block_of, tiles_ref, keep_ref, send_ref, acc_ref, copies=None):
    bundles, slots, rays, cells = tiles_ref.shape
    half = keep_ref.shape[1] - 128
    acc_ref[...] = jnp.zeros_like(acc_ref)
    low = u.astype(BF16)
    for b in range(bundles):
        if copies:
            copies[b].wait()
        rows = low[:, b * rays : (b + 1) * rays]
        for s in range(slots):
            part = jnp.dot(rows, tiles_ref[b, s], preferred_element_type=F32)
            at = pl.multiple_of(block_of(b, s) * cells, cells)
            acc_ref[:, pl.ds(at, cells)] += part
    squares = fold_sq(u, 128)
    for out_ref, at in ((keep_ref, 0), (send_ref, half + cells)):
        out_ref[:, :half] = acc_ref[:, at : at + half]
        out_ref[:, half:] = squares


def first_adjoint(
    pattern_ref, counts_ref, source_u_ref, source_ref, keep_ref, send_ref, tiles_ref, acc_ref,
    u_ref, sem,
):
    bundles = source_ref.shape[0]
    copies = [pltpu.make_async_copy(source_u_ref, u_ref, sem.at[bundles])] + [
        pltpu.make_async_copy(source_ref.at[b], tiles_ref.at[b], sem.at[b])
        for b in range(bundles)
    ]
    for copy in copies:
        copy.start()
    core = lax.axis_index("core")
    blocks = BLK_DEV // 2

    def block_of(b, s):
        found = pattern_ref[b, s]
        upper = (found >= blocks).astype(jnp.int32)
        within = found - blocks * upper
        at = jnp.where(upper == core, within, within + blocks + 1)
        return jnp.where(s < counts_ref[b, 0], at, blocks)

    copies[0].wait()
    scatter_products(u_ref[...], block_of, tiles_ref, keep_ref, send_ref, acc_ref, copies[1:])


def ray_vector(own_ref, left_ref, right_ref, far_ref, prev_ref, beta_ref):
    total = (own_ref[...] + far_ref[...]) + (left_ref[...] + right_ref[...])
    rows = prev_ref.shape[1]
    alpha = jnp.sqrt(lane_sum(total[:, rows:]) + EPS)
    u = total[:, :rows] / alpha - (alpha / beta_ref[:, :1]) * prev_ref[...]
    return u, alpha


def next_adjoint(
    place_ref, own_ref, left_ref, right_ref, far_ref, prev_ref, beta_ref, tiles_ref,
    keep_ref, send_ref, u_ref, alpha_ref, acc_ref,
):
    u, alpha = ray_vector(own_ref, left_ref, right_ref, far_ref, prev_ref, beta_ref)
    u_ref[...] = u
    alpha_ref[...] = wide(alpha)
    slots = tiles_ref.shape[1]
    scatter_products(
        u, lambda b, s: place_ref[b * slots + s], tiles_ref, keep_ref, send_ref, acc_ref
    )


def last_norm(
    own_ref, left_ref, right_ref, far_ref, prev_ref, beta_ref, out_ref, alpha_ref
):
    u, alpha = ray_vector(own_ref, left_ref, right_ref, far_ref, prev_ref, beta_ref)
    alpha_ref[...] = wide(alpha)
    out_ref[...] = fold_sq(u, 128)


def split(value, digits):
    power = jnp.floor(jnp.log2(value))
    return power, value * jnp.exp2(-power) * digits


def pack(keep_ref, other_ref, out_ref):
    total = keep_ref[...] + other_ref[...]
    width = out_ref.shape[1] - 128
    body = total[:, :width]
    peak = jnp.maximum(jnp.max(jnp.abs(body), axis=1, keepdims=True), TINY)
    power, mantissa = split(peak, DIGITS)
    mantissa = jnp.floor(mantissa) + 1.0
    scale = mantissa * jnp.exp2(power) * (1.0 / DIGITS)
    norm_power, norm = split(jnp.maximum(lane_sum(total[:, width:]), TINY), DIGITS)
    high = jnp.floor(norm)
    low = (norm - high) * DIGITS
    lane = lax.broadcasted_iota(jnp.int32, (total.shape[0], 128), 1)
    fields = jnp.zeros_like(lane).astype(F32)
    for at, field in enumerate((power, mantissa, norm_power, high, low)):
        fields = jnp.where(lane == at, field, fields)

    def code(x):
        return jnp.round(x).astype(jnp.int32).astype(jnp.int16)

    out_ref[:, :width] = code(body * (CODES / scale))
    out_ref[:, width:] = code(fields)


def unpack(ref):
    width = ref.shape[1] - 128
    codes = ref[...].astype(jnp.int32).astype(F32)
    power, mantissa, norm_power, high, low = [codes[:, width + at : width + at + 1] for at in range(5)]
    scale = mantissa * jnp.exp2(power) * (1.0 / DIGITS)
    norm = (high + low * (1.0 / DIGITS)) * jnp.exp2(norm_power) * (1.0 / DIGITS)
    return codes[:, :width] * (scale * (1.0 / CODES)), norm


def cell_vector(
    first, own_ref, left_ref, right_ref, far_ref, prev_ref, alpha_ref, v_ref, beta_ref
):
    own, left, right, far = [unpack(ref) for ref in (own_ref, left_ref, right_ref, far_ref)]
    beta = jnp.sqrt((own[1] + far[1]) + (left[1] + right[1]) + EPS)
    v = ((own[0] + far[0]) + (left[0] + right[0])) / beta
    if not first:
        v = v - (beta / alpha_ref[:, :1]) * prev_ref[...]
    v_ref[...] = v
    beta_ref[...] = wide(beta)


def forward(place_ref, own_ref, other_ref, tiles_ref, out_ref, low_ref):
    bundles, slots, rays, cells = tiles_ref.shape
    width = own_ref.shape[1]
    own, other = own_ref[...], other_ref[...]
    low_ref[:, :width] = own.astype(BF16)
    low_ref[:, width : 2 * width] = other.astype(BF16)
    low_ref[:, 2 * width :] = jnp.zeros((own.shape[0], cells), BF16)
    base = bundles * slots
    for b in range(bundles):
        acc = None
        for s in range(slots):
            at = pl.multiple_of(place_ref[base + b * slots + s] * cells, cells)
            part = lax.dot_general(
                low_ref[:, pl.ds(at, cells)], tiles_ref[b, s],
                (((1,), (1,)), ((), ())), preferred_element_type=F32,
            )
            acc = part if acc is None else acc + part
        out_ref[:, b * rays : (b + 1) * rays] = acc
    out_ref[:, bundles * rays :] = fold_sq(own, 128) + fold_sq(other, 128)


def gather_up(*refs):
    count = ITERS
    own_refs, other_refs = refs[:count], refs[count : 2 * count]
    alpha_refs, beta_refs = refs[2 * count : 3 * count], refs[3 * count : 4 * count]
    x_refs, w_refs, phibar_ref, rhobar_ref = refs[4 * count : 4 * count + 2], refs[
        4 * count + 2 : 4 * count + 4], refs[-2], refs[-1]
    alphas = [ref[:, :1] for ref in alpha_refs]
    betas = [ref[:, :1] for ref in beta_refs]
    phibar, rhobar = betas[0], alphas[0]
    steps, turns = [], []
    for k in range(count - 1):
        beta = betas[k + 1]
        rho = jnp.sqrt(rhobar * rhobar + beta * beta)
        cosine, sine = rhobar / rho, beta / rho
        steps.append(cosine * phibar / rho)
        phibar = sine * phibar
        turns.append(sine * alphas[k + 1] / rho)
        rhobar = -cosine * alphas[k + 1]
    for refs, x_ref, w_ref in zip((own_refs, other_refs), x_refs, w_refs):
        w = refs[0][...] / alphas[0]
        x = steps[0] * w
        for k in range(1, count):
            w = refs[k][...] / alphas[k] - turns[k - 1] * w
            if k + 1 < count:
                x = x + steps[k] * w
        x_ref[...] = x
        w_ref[...] = w
    phibar_ref[...] = wide(phibar)
    rhobar_ref[...] = wide(rhobar)


def finish(
    place_ref, own_ref, left_ref, right_ref, far_ref, own_x_ref, other_x_ref, own_w_ref,
    other_w_ref, phibar_ref, rhobar_ref, x_ref, misfit_ref,
):
    width = own_x_ref.shape[1]
    total = (own_ref[...] + far_ref[...]) + (left_ref[...] + right_ref[...])
    beta = jnp.sqrt(lane_sum(total) + EPS)
    phibar, rhobar = phibar_ref[:, :1], rhobar_ref[:, :1]
    rho = jnp.sqrt(rhobar * rhobar + beta * beta)
    step = (rhobar / rho) * phibar / rho
    core = place_ref[place_ref.shape[0] - 1]
    for half, xs_ref, w_ref in ((core, own_x_ref, own_w_ref), (1 - core, other_x_ref, other_w_ref)):
        at = pl.multiple_of(half * width, width)
        x_ref[:, pl.ds(at, width)] = xs_ref[...] + step * w_ref[...]
    last = wide((beta / rho) * phibar)
    row = lax.broadcasted_iota(jnp.int32, last.shape, 0)
    lane = lax.broadcasted_iota(jnp.int32, last.shape, 1)
    misfit_ref[...] = jnp.sum(jnp.where(row == lane, last, 0.0), axis=0, keepdims=True)


def call(body, outs, specs, args, scratch=()):
    return pl.pallas_call(
        body,
        out_shape=outs,
        in_specs=specs,
        out_specs=[VMEM] * len(outs),
        scratch_shapes=list(scratch),
        compiler_params=pltpu.CompilerParams(vmem_limit_bytes=12 << 20),
    )(*args)


def local(right_side, tiles, pattern, counts):
    nrhs, rows = right_side.shape
    bundles, slots, rays, cells = tiles.shape
    blocks = BLK_DEV // 2
    half = blocks * cells
    core = lax.axis_index("core")
    live = lax.broadcasted_iota(jnp.int32, pattern.shape, 1) < counts
    mine = pattern // blocks == core
    within = pattern % blocks
    put = jnp.where(live, jnp.where(mine, within, blocks + 1 + within), blocks)
    get = jnp.where(live, jnp.where(mine, within, blocks + within), BLK_DEV)
    place = jnp.concatenate([put.reshape(-1), get.reshape(-1), core.astype(jnp.int32).reshape(1)])

    def shape(columns, dtype=F32):
        return jax.ShapeDtypeStruct((nrhs, columns), dtype)

    def spread(value, axis):
        n = lax.axis_size(axis)
        moved = [
            lax.ppermute(value, axis, [(i, i ^ by) for i in range(n)]) for by in (1, 3, 2)
        ]
        return [value] + moved

    def swap(value):
        return lax.ppermute(value, "core", [(0, 1), (1, 0)])

    def over_cell(partial):
        own, left, right, far = spread(partial, "x")
        return spread((own + far) + (left + right), "y")

    halves = [shape(half + 128)] * 2
    store = [pltpu.VMEM((nrhs, 2 * (half + cells)), F32)]
    keep, send, tiles = call(
        first_adjoint, halves + [jax.ShapeDtypeStruct(tiles.shape, tiles.dtype)],
        [SMEM, SMEM, HBM, HBM], (
            pattern, counts, pltpu.with_memory_space_constraint(right_side, pltpu.HBM),
            pltpu.with_memory_space_constraint(tiles, pltpu.HBM),
        ),
        store + [pltpu.VMEM(right_side.shape, F32), pltpu.SemaphoreType.DMA((bundles + 1,))],
    )
    u = right_side
    owns, others, alphas, betas = [], [], [], []
    for step in range(ITERS):
        prev = (owns[-1], alphas[-1]) if step else (right_side, right_side)
        packed, = call(
            pack, [shape(half + 128, jnp.int16)], [VMEM] * 2, (keep, swap(send))
        )
        v, beta = call(
            functools.partial(cell_vector, step == 0), [shape(half), shape(128)], [VMEM] * 6,
            (*spread(packed, "z"), *prev),
        )
        other = swap(v)
        owns.append(v)
        others.append(other)
        betas.append(beta)
        products, = call(
            forward, [shape(rows + 128)], [SMEM] + [VMEM] * 3, (place, v, other, tiles),
            [pltpu.VMEM((nrhs, 2 * half + cells), BF16)],
        )
        rows_in = over_cell(products)
        if step + 1 < ITERS:
            keep, send, u, alpha = call(
                next_adjoint, halves + [shape(rows), shape(128)], [SMEM] + [VMEM] * 7,
                (place, *rows_in, u, beta, tiles), store,
            )
        else:
            squares, alpha = call(
                last_norm, [shape(128), shape(128)], [VMEM] * 6, (*rows_in, u, beta)
            )
        alphas.append(alpha)
    so_far = call(
        gather_up, [shape(half)] * 4 + [shape(128)] * 2, [VMEM] * (4 * ITERS),
        (*owns, *others, *alphas, *betas),
    )
    x, misfit = call(
        finish, [shape(2 * half), jax.ShapeDtypeStruct((1, 128), F32)], [SMEM] + [VMEM] * 10,
        (place, *spread(squares + swap(squares), "z"), *so_far),
    )
    return x, misfit[0, :nrhs]


def solution(mesh):
    parts = Mesh(mesh.devices.reshape(4, 2, 4, 4), ("z", "core", "x", "y"))
    ray, cell = ("z", "core"), ("x", "y")
    in_specs = (P(None, ray), P(ray, cell, None, None), P(ray, cell), P(ray, cell))
    out_specs = (P(None, cell), P())
    return jax.shard_map(local, mesh=parts, in_specs=in_specs, out_specs=out_specs, check_vma=False)
```

```python
import functools

import jax
import jax.numpy as jnp
from jax import lax
from jax.experimental import pallas as pl
from jax.experimental.pallas import tpu as pltpu
from jax.sharding import Mesh, PartitionSpec as P

BLK_DEV = 32
ITERS = 4
EPS = 1e-06
TINY = 1e-30
DIGITS = 8192.0
CODES = 32000.0
F32 = jnp.float32
BF16 = jnp.bfloat16

VMEM = pl.BlockSpec(memory_space=pltpu.VMEM)
SMEM = pl.BlockSpec(memory_space=pltpu.SMEM)
HBM = pl.BlockSpec(memory_space=pltpu.HBM)


def lane_sum(x):
    return jnp.sum(x, axis=1, keepdims=True)


def fold_sq(x, width):
    total = None
    for at in range(0, x.shape[1], width):
        piece = x[:, at : at + width]
        total = piece * piece if total is None else total + piece * piece
    return total


def wide(x):
    return jnp.broadcast_to(x, (x.shape[0], 128))


def slots_of(pattern_ref, counts_ref, second, dead):
    blocks = BLK_DEV // 2
    core = lax.axis_index("core")

    def block_of(b, s):
        found = pattern_ref[s, b]
        within = found % blocks
        at = jnp.where(found // blocks == core, within, within + second)
        return jnp.where(s < counts_ref[0, b], at, dead)

    return block_of


def scatter_products(u, block_of, tiles_ref, keep_ref, send_ref, acc_ref, copies=None):
    bundles, slots, rays, cells = tiles_ref.shape
    half = keep_ref.shape[1] - 128
    acc_ref[...] = jnp.zeros_like(acc_ref)
    low = u.astype(BF16)
    for b in range(bundles):
        if copies:
            copies[b].wait()
        rows = low[:, b * rays : (b + 1) * rays]
        for s in range(slots):
            part = jnp.dot(rows, tiles_ref[b, s], preferred_element_type=F32)
            at = pl.multiple_of(block_of(b, s) * cells, cells)
            acc_ref[:, pl.ds(at, cells)] += part
    squares = fold_sq(u, 128)
    for out_ref, at in ((keep_ref, 0), (send_ref, half + cells)):
        out_ref[:, :half] = acc_ref[:, at : at + half]
        out_ref[:, half:] = squares


def first_adjoint(
    source_p_ref, source_c_ref, source_u_ref, source_ref, keep_ref, send_ref, tiles_ref, acc_ref,
    pattern_ref, counts_ref, u_ref, sem,
):
    bundles = source_ref.shape[0]
    small = ((source_p_ref, pattern_ref), (source_c_ref, counts_ref), (source_u_ref, u_ref))
    first = [
        pltpu.make_async_copy(source, target, sem.at[bundles + at])
        for at, (source, target) in enumerate(small)
    ]
    copies = [
        pltpu.make_async_copy(source_ref.at[b], tiles_ref.at[b], sem.at[b])
        for b in range(bundles)
    ]
    for copy in first + copies:
        copy.start()
    for copy in first:
        copy.wait()
    put = slots_of(pattern_ref, counts_ref, BLK_DEV // 2 + 1, BLK_DEV // 2)
    scatter_products(u_ref[...], put, tiles_ref, keep_ref, send_ref, acc_ref, copies)


def ray_vector(own_ref, left_ref, right_ref, far_ref, prev_ref, beta_ref):
    total = (own_ref[...] + far_ref[...]) + (left_ref[...] + right_ref[...])
    rows = prev_ref.shape[1]
    alpha = jnp.sqrt(lane_sum(total[:, rows:]) + EPS)
    u = total[:, :rows] / alpha - (alpha / beta_ref[:, :1]) * prev_ref[...]
    return u, alpha


def next_adjoint(
    pattern_ref, counts_ref, own_ref, left_ref, right_ref, far_ref, prev_ref, beta_ref, tiles_ref,
    keep_ref, send_ref, u_ref, alpha_ref, acc_ref,
):
    u, alpha = ray_vector(own_ref, left_ref, right_ref, far_ref, prev_ref, beta_ref)
    u_ref[...] = u
    alpha_ref[...] = wide(alpha)
    put = slots_of(pattern_ref, counts_ref, BLK_DEV // 2 + 1, BLK_DEV // 2)
    scatter_products(u, put, tiles_ref, keep_ref, send_ref, acc_ref)


def last_norm(
    own_ref, left_ref, right_ref, far_ref, prev_ref, beta_ref, out_ref, alpha_ref
):
    u, alpha = ray_vector(own_ref, left_ref, right_ref, far_ref, prev_ref, beta_ref)
    alpha_ref[...] = wide(alpha)
    out_ref[...] = fold_sq(u, 128)


def split(value, digits):
    power = jnp.floor(jnp.log2(value))
    return power, value * jnp.exp2(-power) * digits


def pack(keep_ref, other_ref, out_ref):
    total = keep_ref[...] + other_ref[...]
    width = out_ref.shape[1] - 128
    body = total[:, :width]
    peak = jnp.maximum(jnp.max(jnp.abs(body), axis=1, keepdims=True), TINY)
    power, mantissa = split(peak, DIGITS)
    mantissa = jnp.floor(mantissa) + 1.0
    scale = mantissa * jnp.exp2(power) * (1.0 / DIGITS)
    norm_power, norm = split(jnp.maximum(lane_sum(total[:, width:]), TINY), DIGITS)
    high = jnp.floor(norm)
    low = (norm - high) * DIGITS
    lane = lax.broadcasted_iota(jnp.int32, (total.shape[0], 128), 1)
    fields = jnp.zeros_like(lane).astype(F32)
    for at, field in enumerate((power, mantissa, norm_power, high, low)):
        fields = jnp.where(lane == at, field, fields)

    def code(x):
        return jnp.round(x).astype(jnp.int32).astype(jnp.int16)

    out_ref[:, :width] = code(body * (CODES / scale))
    out_ref[:, width:] = code(fields)


def unpack(ref):
    width = ref.shape[1] - 128
    codes = ref[...].astype(jnp.int32).astype(F32)
    power, mantissa, norm_power, high, low = [codes[:, width + at : width + at + 1] for at in range(5)]
    scale = mantissa * jnp.exp2(power) * (1.0 / DIGITS)
    norm = (high + low * (1.0 / DIGITS)) * jnp.exp2(norm_power) * (1.0 / DIGITS)
    return codes[:, :width] * (scale * (1.0 / CODES)), norm


def cell_vector(
    first, own_ref, left_ref, right_ref, far_ref, prev_ref, alpha_ref, v_ref, beta_ref
):
    own, left, right, far = [unpack(ref) for ref in (own_ref, left_ref, right_ref, far_ref)]
    beta = jnp.sqrt((own[1] + far[1]) + (left[1] + right[1]) + EPS)
    v = ((own[0] + far[0]) + (left[0] + right[0])) / beta
    if not first:
        v = v - (beta / alpha_ref[:, :1]) * prev_ref[...]
    v_ref[...] = v
    beta_ref[...] = wide(beta)


def forward(pattern_ref, counts_ref, own_ref, other_ref, tiles_ref, out_ref, low_ref):
    bundles, slots, rays, cells = tiles_ref.shape
    width = own_ref.shape[1]
    own, other = own_ref[...], other_ref[...]
    low_ref[:, :width] = own.astype(BF16)
    low_ref[:, width : 2 * width] = other.astype(BF16)
    low_ref[:, 2 * width :] = jnp.zeros((own.shape[0], cells), BF16)
    get = slots_of(pattern_ref, counts_ref, BLK_DEV // 2, BLK_DEV)
    for b in range(bundles):
        acc = None
        for s in range(slots):
            at = pl.multiple_of(get(b, s) * cells, cells)
            part = lax.dot_general(
                low_ref[:, pl.ds(at, cells)], tiles_ref[b, s],
                (((1,), (1,)), ((), ())), preferred_element_type=F32,
            )
            acc = part if acc is None else acc + part
        out_ref[:, b * rays : (b + 1) * rays] = acc
    out_ref[:, bundles * rays :] = fold_sq(own, 128) + fold_sq(other, 128)


def gather_up(*refs):
    count = ITERS
    own_refs, other_refs = refs[:count], refs[count : 2 * count]
    alpha_refs, beta_refs = refs[2 * count : 3 * count], refs[3 * count : 4 * count]
    x_refs, w_refs, phibar_ref, rhobar_ref = refs[4 * count : 4 * count + 2], refs[
        4 * count + 2 : 4 * count + 4], refs[-2], refs[-1]
    alphas = [ref[:, :1] for ref in alpha_refs]
    betas = [ref[:, :1] for ref in beta_refs]
    phibar, rhobar = betas[0], alphas[0]
    steps, turns = [], []
    for k in range(count - 1):
        beta = betas[k + 1]
        rho = jnp.sqrt(rhobar * rhobar + beta * beta)
        cosine, sine = rhobar / rho, beta / rho
        steps.append(cosine * phibar / rho)
        phibar = sine * phibar
        turns.append(sine * alphas[k + 1] / rho)
        rhobar = -cosine * alphas[k + 1]
    for refs, x_ref, w_ref in zip((own_refs, other_refs), x_refs, w_refs):
        w = refs[0][...] / alphas[0]
        x = steps[0] * w
        for k in range(1, count):
            w = refs[k][...] / alphas[k] - turns[k - 1] * w
            if k + 1 < count:
                x = x + steps[k] * w
        x_ref[...] = x
        w_ref[...] = w
    phibar_ref[...] = wide(phibar)
    rhobar_ref[...] = wide(rhobar)


def finish(
    own_ref, left_ref, right_ref, far_ref, own_x_ref, other_x_ref, own_w_ref,
    other_w_ref, phibar_ref, rhobar_ref, x_ref, misfit_ref,
):
    width = own_x_ref.shape[1]
    total = (own_ref[...] + far_ref[...]) + (left_ref[...] + right_ref[...])
    beta = jnp.sqrt(lane_sum(total) + EPS)
    phibar, rhobar = phibar_ref[:, :1], rhobar_ref[:, :1]
    rho = jnp.sqrt(rhobar * rhobar + beta * beta)
    step = (rhobar / rho) * phibar / rho
    core = lax.axis_index("core")
    for half, xs_ref, w_ref in ((core, own_x_ref, own_w_ref), (1 - core, other_x_ref, other_w_ref)):
        at = pl.multiple_of(half * width, width)
        x_ref[:, pl.ds(at, width)] = xs_ref[...] + step * w_ref[...]
    last = wide((beta / rho) * phibar)
    row = lax.broadcasted_iota(jnp.int32, last.shape, 0)
    lane = lax.broadcasted_iota(jnp.int32, last.shape, 1)
    across = jnp.sum(jnp.where(row == lane, last, 0.0), axis=0, keepdims=True)
    misfit_ref[...] = across[:, : misfit_ref.shape[1]]


def call(body, outs, specs, args, scratch=()):
    return pl.pallas_call(
        body,
        out_shape=outs,
        in_specs=specs,
        out_specs=[VMEM] * len(outs),
        scratch_shapes=list(scratch),
        compiler_params=pltpu.CompilerParams(vmem_limit_bytes=12 << 20),
    )(*args)


def local(right_side, tiles, pattern, counts):
    nrhs, rows = right_side.shape
    bundles, slots, rays, cells = tiles.shape
    blocks = BLK_DEV // 2
    half = blocks * cells
    slots_in = (pattern.T, counts.T)

    def shape(columns, dtype=F32):
        return jax.ShapeDtypeStruct((nrhs, columns), dtype)

    def spread(value, axis):
        n = lax.axis_size(axis)
        moved = [
            lax.ppermute(value, axis, [(i, i ^ by) for i in range(n)]) for by in (1, 3, 2)
        ]
        return [value] + moved

    def swap(value):
        return lax.ppermute(value, "core", [(0, 1), (1, 0)])

    def over_cell(partial):
        own, left, right, far = spread(partial, "x")
        return spread((own + far) + (left + right), "y")

    halves = [shape(half + 128)] * 2
    store = [pltpu.VMEM((nrhs, 2 * (half + cells)), F32)]
    keep, send, tiles = call(
        first_adjoint, halves + [jax.ShapeDtypeStruct(tiles.shape, tiles.dtype)],
        [HBM] * 4,
        [pltpu.with_memory_space_constraint(z, pltpu.HBM) for z in (*slots_in, right_side, tiles)],
        store + [
            pltpu.SMEM((slots, bundles), jnp.int32), pltpu.SMEM((1, bundles), jnp.int32),
            pltpu.VMEM(right_side.shape, F32), pltpu.SemaphoreType.DMA((bundles + 3,)),
        ],
    )
    u = right_side
    owns, others, alphas, betas = [], [], [], []
    for step in range(ITERS):
        prev = (owns[-1], alphas[-1]) if step else (right_side, right_side)
        packed, = call(
            pack, [shape(half + 128, jnp.int16)], [VMEM] * 2, (keep, swap(send))
        )
        v, beta = call(
            functools.partial(cell_vector, step == 0), [shape(half), shape(128)], [VMEM] * 6,
            (*spread(packed, "z"), *prev),
        )
        other = swap(v)
        owns.append(v)
        others.append(other)
        betas.append(beta)
        products, = call(
            forward, [shape(rows + 128)], [SMEM] * 2 + [VMEM] * 3, (*slots_in, v, other, tiles),
            [pltpu.VMEM((nrhs, 2 * half + cells), BF16)],
        )
        rows_in = over_cell(products)
        if step + 1 < ITERS:
            keep, send, u, alpha = call(
                next_adjoint, halves + [shape(rows), shape(128)], [SMEM] * 2 + [VMEM] * 7,
                (*slots_in, *rows_in, u, beta, tiles), store,
            )
        else:
            squares, alpha = call(
                last_norm, [shape(128), shape(128)], [VMEM] * 6, (*rows_in, u, beta)
            )
        alphas.append(alpha)
    so_far = call(
        gather_up, [shape(half)] * 4 + [shape(128)] * 2, [VMEM] * (4 * ITERS),
        (*owns, *others, *alphas, *betas),
    )
    x, misfit = call(
        finish, [shape(2 * half), jax.ShapeDtypeStruct((1, nrhs), F32)], [VMEM] * 10,
        (*spread(squares + swap(squares), "z"), *so_far),
    )
    return x, misfit.reshape(nrhs)


def solution(mesh):
    parts = Mesh(mesh.devices.reshape(4, 2, 4, 4), ("z", "core", "x", "y"))
    ray, cell = ("z", "core"), ("x", "y")
    in_specs = (P(None, ray), P(ray, cell, None, None), P(ray, cell), P(ray, cell))
    out_specs = (P(None, cell), P())
    return jax.shard_map(local, mesh=parts, in_specs=in_specs, out_specs=out_specs, check_vma=False)
```

```python
import functools

import jax
import jax.numpy as jnp
from jax import lax
from jax.experimental import pallas as pl
from jax.experimental.pallas import tpu as pltpu
from jax.sharding import Mesh, PartitionSpec as P

BLK_DEV = 32
ITERS = 4
EPS = 1e-06
TINY = 1e-30
DIGITS = 8192.0
CODES = 32000.0
F32 = jnp.float32
BF16 = jnp.bfloat16

VMEM = pl.BlockSpec(memory_space=pltpu.VMEM)
SMEM = pl.BlockSpec(memory_space=pltpu.SMEM)
HBM = pl.BlockSpec(memory_space=pltpu.HBM)


def lane_sum(x):
    return jnp.sum(x, axis=1, keepdims=True)


def fold_sq(x, width):
    total = None
    for at in range(0, x.shape[1], width):
        piece = x[:, at : at + width]
        total = piece * piece if total is None else total + piece * piece
    return total


def wide(x):
    return jnp.broadcast_to(x, (x.shape[0], 128))


def slots_of(pattern_ref, counts_ref, second, dead):
    blocks = BLK_DEV // 2
    core = lax.axis_index("core")

    def block_of(b, s):
        found = pattern_ref[s, b]
        within = found % blocks
        at = jnp.where(found // blocks == core, within, within + second)
        return jnp.where(s < counts_ref[0, b], at, dead)

    return block_of


def scatter_products(u, block_of, tiles_ref, keep_ref, send_ref, acc_ref, copies=None):
    bundles, slots, rays, cells = tiles_ref.shape
    half = keep_ref.shape[1] - 128
    acc_ref[...] = jnp.zeros_like(acc_ref)
    low = u.astype(BF16)
    for b in range(bundles):
        if copies:
            copies[b].wait()
        rows = low[:, b * rays : (b + 1) * rays]
        for s in range(slots):
            part = jnp.dot(rows, tiles_ref[b, s], preferred_element_type=F32)
            at = pl.multiple_of(block_of(b, s) * cells, cells)
            acc_ref[:, pl.ds(at, cells)] += part
    squares = fold_sq(u, 128)
    for out_ref, at in ((keep_ref, 0), (send_ref, half + cells)):
        out_ref[:, :half] = acc_ref[:, at : at + half]
        out_ref[:, half:] = squares


def first_adjoint(
    source_p_ref, source_c_ref, source_u_ref, source_ref, keep_ref, send_ref, tiles_ref, acc_ref,
    pattern_ref, counts_ref, u_ref, sem,
):
    bundles = source_ref.shape[0]
    small = ((source_p_ref, pattern_ref), (source_c_ref, counts_ref), (source_u_ref, u_ref))
    first = [
        pltpu.make_async_copy(source, target, sem.at[bundles + at])
        for at, (source, target) in enumerate(small)
    ]
    copies = [
        pltpu.make_async_copy(source_ref.at[b], tiles_ref.at[b], sem.at[b])
        for b in range(bundles)
    ]
    for copy in first + copies:
        copy.start()
    for copy in first:
        copy.wait()
    put = slots_of(pattern_ref, counts_ref, BLK_DEV // 2 + 1, BLK_DEV // 2)
    scatter_products(u_ref[...], put, tiles_ref, keep_ref, send_ref, acc_ref, copies)


def ray_vector(own_ref, left_ref, right_ref, far_ref, prev_ref, beta_ref):
    total = (own_ref[...] + far_ref[...]) + (left_ref[...] + right_ref[...])
    rows = prev_ref.shape[1]
    alpha = jnp.sqrt(lane_sum(total[:, rows:]) + EPS)
    u = total[:, :rows] / alpha - (alpha / beta_ref[:, :1]) * prev_ref[...]
    return u, alpha


def next_adjoint(
    pattern_ref, counts_ref, own_ref, left_ref, right_ref, far_ref, prev_ref, beta_ref, tiles_ref,
    keep_ref, send_ref, u_ref, alpha_ref, acc_ref,
):
    u, alpha = ray_vector(own_ref, left_ref, right_ref, far_ref, prev_ref, beta_ref)
    u_ref[...] = u
    alpha_ref[...] = wide(alpha)
    put = slots_of(pattern_ref, counts_ref, BLK_DEV // 2 + 1, BLK_DEV // 2)
    scatter_products(u, put, tiles_ref, keep_ref, send_ref, acc_ref)


def last_norm(
    own_ref, left_ref, right_ref, far_ref, prev_ref, beta_ref, out_ref, alpha_ref
):
    u, alpha = ray_vector(own_ref, left_ref, right_ref, far_ref, prev_ref, beta_ref)
    alpha_ref[...] = wide(alpha)
    out_ref[...] = fold_sq(u, 128)


def split(value, digits):
    power = jnp.floor(jnp.log2(value))
    return power, value * jnp.exp2(-power) * digits


def pack(keep_ref, other_ref, out_ref):
    total = keep_ref[...] + other_ref[...]
    width = out_ref.shape[1] - 128
    body = total[:, :width]
    peak = jnp.maximum(jnp.max(jnp.abs(body), axis=1, keepdims=True), TINY)
    power, mantissa = split(peak, DIGITS)
    mantissa = jnp.floor(mantissa) + 1.0
    scale = mantissa * jnp.exp2(power) * (1.0 / DIGITS)
    norm_power, norm = split(jnp.maximum(lane_sum(total[:, width:]), TINY), DIGITS)
    high = jnp.floor(norm)
    low = (norm - high) * DIGITS
    lane = lax.broadcasted_iota(jnp.int32, (total.shape[0], 128), 1)
    fields = jnp.zeros_like(lane).astype(F32)
    for at, field in enumerate((power, mantissa, norm_power, high, low)):
        fields = jnp.where(lane == at, field, fields)

    def code(x):
        return jnp.round(x).astype(jnp.int32).astype(jnp.int16)

    out_ref[:, :width] = code(body * (CODES / scale))
    out_ref[:, width:] = code(fields)


def unpack(ref):
    width = ref.shape[1] - 128
    codes = ref[...].astype(jnp.int32).astype(F32)
    power, mantissa, norm_power, high, low = [codes[:, width + at : width + at + 1] for at in range(5)]
    scale = mantissa * jnp.exp2(power) * (1.0 / DIGITS)
    norm = (high + low * (1.0 / DIGITS)) * jnp.exp2(norm_power) * (1.0 / DIGITS)
    return codes[:, :width] * (scale * (1.0 / CODES)), norm


def cell_vector(
    first, own_ref, left_ref, right_ref, far_ref, prev_ref, alpha_ref, v_ref, beta_ref
):
    own, left, right, far = [unpack(ref) for ref in (own_ref, left_ref, right_ref, far_ref)]
    beta = jnp.sqrt((own[1] + far[1]) + (left[1] + right[1]) + EPS)
    v = ((own[0] + far[0]) + (left[0] + right[0])) / beta
    if not first:
        v = v - (beta / alpha_ref[:, :1]) * prev_ref[...]
    v_ref[...] = v
    beta_ref[...] = wide(beta)


def turn(tiles_ref, out_ref):
    for b in range(tiles_ref.shape[0]):
        for s in range(tiles_ref.shape[1]):
            out_ref[b, s] = tiles_ref[b, s].T


def forward(pattern_ref, counts_ref, own_ref, other_ref, tiles_ref, out_ref, low_ref):
    bundles, slots, cells, rays = tiles_ref.shape
    width = own_ref.shape[1]
    own, other = own_ref[...], other_ref[...]
    low_ref[:, :width] = own.astype(BF16)
    low_ref[:, width : 2 * width] = other.astype(BF16)
    low_ref[:, 2 * width :] = jnp.zeros((own.shape[0], cells), BF16)
    get = slots_of(pattern_ref, counts_ref, BLK_DEV // 2, BLK_DEV)
    for b in range(bundles):
        acc = None
        for s in range(slots):
            at = pl.multiple_of(get(b, s) * cells, cells)
            part = jnp.dot(
                low_ref[:, pl.ds(at, cells)], tiles_ref[b, s], preferred_element_type=F32
            )
            acc = part if acc is None else acc + part
        out_ref[:, b * rays : (b + 1) * rays] = acc
    out_ref[:, bundles * rays :] = fold_sq(own, 128) + fold_sq(other, 128)


def gather_up(*refs):
    count = ITERS
    own_refs, other_refs = refs[:count], refs[count : 2 * count]
    alpha_refs, beta_refs = refs[2 * count : 3 * count], refs[3 * count : 4 * count]
    x_refs, w_refs, phibar_ref, rhobar_ref = refs[4 * count : 4 * count + 2], refs[
        4 * count + 2 : 4 * count + 4], refs[-2], refs[-1]
    alphas = [ref[:, :1] for ref in alpha_refs]
    betas = [ref[:, :1] for ref in beta_refs]
    phibar, rhobar = betas[0], alphas[0]
    steps, turns = [], []
    for k in range(count - 1):
        beta = betas[k + 1]
        rho = jnp.sqrt(rhobar * rhobar + beta * beta)
        cosine, sine = rhobar / rho, beta / rho
        steps.append(cosine * phibar / rho)
        phibar = sine * phibar
        turns.append(sine * alphas[k + 1] / rho)
        rhobar = -cosine * alphas[k + 1]
    for refs, x_ref, w_ref in zip((own_refs, other_refs), x_refs, w_refs):
        w = refs[0][...] / alphas[0]
        x = steps[0] * w
        for k in range(1, count):
            w = refs[k][...] / alphas[k] - turns[k - 1] * w
            if k + 1 < count:
                x = x + steps[k] * w
        x_ref[...] = x
        w_ref[...] = w
    phibar_ref[...] = wide(phibar)
    rhobar_ref[...] = wide(rhobar)


def finish(
    own_ref, left_ref, right_ref, far_ref, own_x_ref, other_x_ref, own_w_ref,
    other_w_ref, phibar_ref, rhobar_ref, x_ref, misfit_ref,
):
    width = own_x_ref.shape[1]
    total = (own_ref[...] + far_ref[...]) + (left_ref[...] + right_ref[...])
    beta = jnp.sqrt(lane_sum(total) + EPS)
    phibar, rhobar = phibar_ref[:, :1], rhobar_ref[:, :1]
    rho = jnp.sqrt(rhobar * rhobar + beta * beta)
    step = (rhobar / rho) * phibar / rho
    core = lax.axis_index("core")
    for half, xs_ref, w_ref in ((core, own_x_ref, own_w_ref), (1 - core, other_x_ref, other_w_ref)):
        at = pl.multiple_of(half * width, width)
        x_ref[:, pl.ds(at, width)] = xs_ref[...] + step * w_ref[...]
    last = wide((beta / rho) * phibar)
    row = lax.broadcasted_iota(jnp.int32, last.shape, 0)
    lane = lax.broadcasted_iota(jnp.int32, last.shape, 1)
    across = jnp.sum(jnp.where(row == lane, last, 0.0), axis=0, keepdims=True)
    misfit_ref[...] = across[:, : misfit_ref.shape[1]]


def call(body, outs, specs, args, scratch=()):
    return pl.pallas_call(
        body,
        out_shape=outs,
        in_specs=specs,
        out_specs=[VMEM] * len(outs),
        scratch_shapes=list(scratch),
        compiler_params=pltpu.CompilerParams(vmem_limit_bytes=12 << 20),
    )(*args)


def local(right_side, tiles, pattern, counts):
    nrhs, rows = right_side.shape
    bundles, slots, rays, cells = tiles.shape
    blocks = BLK_DEV // 2
    half = blocks * cells
    slots_in = (pattern.T, counts.T)

    def shape(columns, dtype=F32):
        return jax.ShapeDtypeStruct((nrhs, columns), dtype)

    def spread(value, axis):
        n = lax.axis_size(axis)
        moved = [
            lax.ppermute(value, axis, [(i, i ^ by) for i in range(n)]) for by in (1, 3, 2)
        ]
        return [value] + moved

    def swap(value):
        return lax.ppermute(value, "core", [(0, 1), (1, 0)])

    def over_cell(partial):
        own, left, right, far = spread(partial, "x")
        return spread((own + far) + (left + right), "y")

    halves = [shape(half + 128)] * 2
    store = [pltpu.VMEM((nrhs, 2 * (half + cells)), F32)]
    keep, send, tiles = call(
        first_adjoint, halves + [jax.ShapeDtypeStruct(tiles.shape, tiles.dtype)],
        [HBM] * 4,
        [pltpu.with_memory_space_constraint(z, pltpu.HBM) for z in (*slots_in, right_side, tiles)],
        store + [
            pltpu.SMEM((slots, bundles), jnp.int32), pltpu.SMEM((1, bundles), jnp.int32),
            pltpu.VMEM(right_side.shape, F32), pltpu.SemaphoreType.DMA((bundles + 3,)),
        ],
    )
    turned, = call(
        turn, [jax.ShapeDtypeStruct((bundles, slots, cells, rays), tiles.dtype)], [VMEM], (tiles,)
    )
    u = right_side
    owns, others, alphas, betas = [], [], [], []
    for step in range(ITERS):
        prev = (owns[-1], alphas[-1]) if step else (right_side, right_side)
        packed, = call(
            pack, [shape(half + 128, jnp.int16)], [VMEM] * 2, (keep, swap(send))
        )
        v, beta = call(
            functools.partial(cell_vector, step == 0), [shape(half), shape(128)], [VMEM] * 6,
            (*spread(packed, "z"), *prev),
        )
        other = swap(v)
        owns.append(v)
        others.append(other)
        betas.append(beta)
        products, = call(
            forward, [shape(rows + 128)], [SMEM] * 2 + [VMEM] * 3, (*slots_in, v, other, turned),
            [pltpu.VMEM((nrhs, 2 * half + cells), BF16)],
        )
        rows_in = over_cell(products)
        if step + 1 < ITERS:
            keep, send, u, alpha = call(
                next_adjoint, halves + [shape(rows), shape(128)], [SMEM] * 2 + [VMEM] * 7,
                (*slots_in, *rows_in, u, beta, tiles), store,
            )
        else:
            squares, alpha = call(
                last_norm, [shape(128), shape(128)], [VMEM] * 6, (*rows_in, u, beta)
            )
        alphas.append(alpha)
    so_far = call(
        gather_up, [shape(half)] * 4 + [shape(128)] * 2, [VMEM] * (4 * ITERS),
        (*owns, *others, *alphas, *betas),
    )
    x, misfit = call(
        finish, [shape(2 * half), jax.ShapeDtypeStruct((1, nrhs), F32)], [VMEM] * 10,
        (*spread(squares + swap(squares), "z"), *so_far),
    )
    return x, misfit.reshape(nrhs)


def solution(mesh):
    parts = Mesh(mesh.devices.reshape(4, 2, 4, 4), ("z", "core", "x", "y"))
    ray, cell = ("z", "core"), ("x", "y")
    in_specs = (P(None, ray), P(ray, cell, None, None), P(ray, cell), P(ray, cell))
    out_specs = (P(None, cell), P())
    return jax.shard_map(local, mesh=parts, in_specs=in_specs, out_specs=out_specs, check_vma=False)
```

```python
import functools

import jax
import jax.numpy as jnp
from jax import lax
from jax.experimental import pallas as pl
from jax.experimental.pallas import tpu as pltpu
from jax.sharding import Mesh, PartitionSpec as P

BLK_DEV = 32
ITERS = 4
EPS = 1e-06
TINY = 1e-30
DIGITS = 8192.0
CODES = 32000.0
F32 = jnp.float32
BF16 = jnp.bfloat16

VMEM = pl.BlockSpec(memory_space=pltpu.VMEM)
SMEM = pl.BlockSpec(memory_space=pltpu.SMEM)
HBM = pl.BlockSpec(memory_space=pltpu.HBM)


def lane_sum(x):
    return jnp.sum(x, axis=1, keepdims=True)


def fold_sq(x, width):
    total = None
    for at in range(0, x.shape[1], width):
        piece = x[:, at : at + width]
        total = piece * piece if total is None else total + piece * piece
    return total


def wide(x):
    return jnp.broadcast_to(x, (x.shape[0], 128))


def slots_of(pattern_ref, counts_ref, second, dead):
    blocks = BLK_DEV // 2
    core = lax.axis_index("core")

    def block_of(b, s):
        found = pattern_ref[s, b]
        within = found % blocks
        at = jnp.where(found // blocks == core, within, within + second)
        return jnp.where(s < counts_ref[0, b], at, dead)

    return block_of


def scatter_products(u, block_of, tiles_ref, keep_ref, send_ref, acc_ref, copies=None):
    bundles, slots, rays, cells = tiles_ref.shape
    half = keep_ref.shape[1] - 128
    acc_ref[...] = jnp.zeros_like(acc_ref)
    low = u.astype(BF16)
    for b in range(bundles):
        if copies:
            copies[b].wait()
        rows = low[:, b * rays : (b + 1) * rays]
        for s in range(slots):
            part = jnp.dot(rows, tiles_ref[b, s], preferred_element_type=F32)
            at = pl.multiple_of(block_of(b, s) * cells, cells)
            acc_ref[:, pl.ds(at, cells)] += part
    squares = fold_sq(u, 128)
    for out_ref, at in ((keep_ref, 0), (send_ref, half + cells)):
        out_ref[:, :half] = acc_ref[:, at : at + half]
        out_ref[:, half:] = squares


def first_adjoint(
    source_p_ref, source_c_ref, source_u_ref, source_ref, keep_ref, send_ref, tiles_ref, acc_ref,
    pattern_ref, counts_ref, u_ref, sem,
):
    bundles = source_ref.shape[0]
    small = ((source_p_ref, pattern_ref), (source_c_ref, counts_ref), (source_u_ref, u_ref))
    first = [
        pltpu.make_async_copy(source, target, sem.at[bundles + at])
        for at, (source, target) in enumerate(small)
    ]
    copies = [
        pltpu.make_async_copy(source_ref.at[b], tiles_ref.at[b], sem.at[b])
        for b in range(bundles)
    ]
    for copy in first + copies:
        copy.start()
    for copy in first:
        copy.wait()
    put = slots_of(pattern_ref, counts_ref, BLK_DEV // 2 + 1, BLK_DEV // 2)
    scatter_products(u_ref[...], put, tiles_ref, keep_ref, send_ref, acc_ref, copies)


def ray_vector(own_ref, left_ref, right_ref, far_ref, prev_ref, beta_ref):
    total = (own_ref[...] + far_ref[...]) + (left_ref[...] + right_ref[...])
    rows = prev_ref.shape[1]
    alpha = jnp.sqrt(lane_sum(total[:, rows:]) + EPS)
    u = total[:, :rows] / alpha - (alpha / beta_ref[:, :1]) * prev_ref[...]
    return u, alpha


def next_adjoint(
    pattern_ref, counts_ref, own_ref, left_ref, right_ref, far_ref, prev_ref, beta_ref, tiles_ref,
    keep_ref, send_ref, u_ref, alpha_ref, acc_ref,
):
    u, alpha = ray_vector(own_ref, left_ref, right_ref, far_ref, prev_ref, beta_ref)
    u_ref[...] = u
    alpha_ref[...] = wide(alpha)
    put = slots_of(pattern_ref, counts_ref, BLK_DEV // 2 + 1, BLK_DEV // 2)
    scatter_products(u, put, tiles_ref, keep_ref, send_ref, acc_ref)


def last_norm(
    own_ref, left_ref, right_ref, far_ref, prev_ref, beta_ref, out_ref, alpha_ref
):
    u, alpha = ray_vector(own_ref, left_ref, right_ref, far_ref, prev_ref, beta_ref)
    alpha_ref[...] = wide(alpha)
    out_ref[...] = fold_sq(u, 128)


def split(value, digits):
    power = jnp.floor(jnp.log2(value))
    return power, value * jnp.exp2(-power) * digits


def pack(keep_ref, other_ref, out_ref):
    total = keep_ref[...] + other_ref[...]
    width = out_ref.shape[1] - 128
    body = total[:, :width]
    peak = jnp.maximum(jnp.max(jnp.abs(body), axis=1, keepdims=True), TINY)
    power, mantissa = split(peak, DIGITS)
    mantissa = jnp.floor(mantissa) + 1.0
    scale = mantissa * jnp.exp2(power) * (1.0 / DIGITS)
    norm_power, norm = split(jnp.maximum(lane_sum(total[:, width:]), TINY), DIGITS)
    high = jnp.floor(norm)
    low = (norm - high) * DIGITS
    lane = lax.broadcasted_iota(jnp.int32, (total.shape[0], 128), 1)
    fields = jnp.zeros_like(lane).astype(F32)
    for at, field in enumerate((power, mantissa, norm_power, high, low)):
        fields = jnp.where(lane == at, field, fields)

    def code(x):
        return jnp.round(x).astype(jnp.int32).astype(jnp.int16)

    out_ref[:, :width] = code(body * (CODES / scale))
    out_ref[:, width:] = code(fields)


def unpack(ref):
    width = ref.shape[1] - 128
    codes = ref[...].astype(jnp.int32).astype(F32)
    power, mantissa, norm_power, high, low = [codes[:, width + at : width + at + 1] for at in range(5)]
    scale = mantissa * jnp.exp2(power) * (1.0 / DIGITS)
    norm = (high + low * (1.0 / DIGITS)) * jnp.exp2(norm_power) * (1.0 / DIGITS)
    return codes[:, :width] * (scale * (1.0 / CODES)), norm


def cell_vector(
    first, own_ref, left_ref, right_ref, far_ref, prev_ref, alpha_ref, v_ref, beta_ref
):
    own, left, right, far = [unpack(ref) for ref in (own_ref, left_ref, right_ref, far_ref)]
    beta = jnp.sqrt((own[1] + far[1]) + (left[1] + right[1]) + EPS)
    v = ((own[0] + far[0]) + (left[0] + right[0])) / beta
    if not first:
        v = v - (beta / alpha_ref[:, :1]) * prev_ref[...]
    v_ref[...] = v
    beta_ref[...] = wide(beta)


def turn(tiles_ref, out_ref):
    for b in range(tiles_ref.shape[0]):
        for s in range(tiles_ref.shape[1]):
            out_ref[b, s] = tiles_ref[b, s].T


def forward(pattern_ref, counts_ref, own_ref, other_ref, tiles_ref, out_ref, low_ref):
    bundles, slots, cells, rays = tiles_ref.shape
    width = own_ref.shape[1]
    own, other = own_ref[...], other_ref[...]
    low_ref[:, :width] = own.astype(BF16)
    low_ref[:, width : 2 * width] = other.astype(BF16)
    low_ref[:, 2 * width :] = jnp.zeros((own.shape[0], cells), BF16)
    get = slots_of(pattern_ref, counts_ref, BLK_DEV // 2, BLK_DEV)
    for b in range(bundles):
        acc = None
        for s in range(slots):
            at = pl.multiple_of(get(b, s) * cells, cells)
            part = jnp.dot(
                low_ref[:, pl.ds(at, cells)], tiles_ref[b, s], preferred_element_type=F32
            )
            acc = part if acc is None else acc + part
        out_ref[:, b * rays : (b + 1) * rays] = acc
    out_ref[:, bundles * rays :] = fold_sq(own, 128) + fold_sq(other, 128)


def gather_up(*refs):
    count = ITERS
    own_refs, other_refs = refs[:count], refs[count : 2 * count]
    alpha_refs, beta_refs = refs[2 * count : 3 * count], refs[3 * count : 4 * count]
    x_refs, w_refs, phibar_ref, rhobar_ref = refs[4 * count : 4 * count + 2], refs[
        4 * count + 2 : 4 * count + 4], refs[-2], refs[-1]
    alphas = [ref[:, :1] for ref in alpha_refs]
    betas = [ref[:, :1] for ref in beta_refs]
    phibar, rhobar = betas[0], alphas[0]
    steps, turns = [], []
    for k in range(count - 1):
        beta = betas[k + 1]
        rho = jnp.sqrt(rhobar * rhobar + beta * beta)
        cosine, sine = rhobar / rho, beta / rho
        steps.append(cosine * phibar / rho)
        phibar = sine * phibar
        turns.append(sine * alphas[k + 1] / rho)
        rhobar = -cosine * alphas[k + 1]
    for refs, x_ref, w_ref in zip((own_refs, other_refs), x_refs, w_refs):
        w = refs[0][...] / alphas[0]
        x = steps[0] * w
        for k in range(1, count):
            w = refs[k][...] / alphas[k] - turns[k - 1] * w
            if k + 1 < count:
                x = x + steps[k] * w
        x_ref[...] = x
        w_ref[...] = w
    phibar_ref[...] = wide(phibar)
    rhobar_ref[...] = wide(rhobar)


def finish(
    own_ref, left_ref, right_ref, far_ref, own_x_ref, other_x_ref, own_w_ref,
    other_w_ref, phibar_ref, rhobar_ref, x_ref, misfit_ref,
):
    width = own_x_ref.shape[1]
    total = (own_ref[...] + far_ref[...]) + (left_ref[...] + right_ref[...])
    beta = jnp.sqrt(lane_sum(total) + EPS)
    phibar, rhobar = phibar_ref[:, :1], rhobar_ref[:, :1]
    rho = jnp.sqrt(rhobar * rhobar + beta * beta)
    step = (rhobar / rho) * phibar / rho
    core = lax.axis_index("core")
    for half, xs_ref, w_ref in ((core, own_x_ref, own_w_ref), (1 - core, other_x_ref, other_w_ref)):
        at = pl.multiple_of(half * width, width)
        x_ref[:, pl.ds(at, width)] = xs_ref[...] + step * w_ref[...]
    last = wide((beta / rho) * phibar)
    row = lax.broadcasted_iota(jnp.int32, last.shape, 0)
    lane = lax.broadcasted_iota(jnp.int32, last.shape, 1)
    across = jnp.sum(jnp.where(row == lane, last, 0.0), axis=0, keepdims=True)
    misfit_ref[...] = across[:, : misfit_ref.shape[1]]


def call(body, outs, specs, args, scratch=()):
    return pl.pallas_call(
        body,
        out_shape=outs,
        in_specs=specs,
        out_specs=[VMEM] * len(outs),
        scratch_shapes=list(scratch),
        compiler_params=pltpu.CompilerParams(vmem_limit_bytes=12 << 20),
    )(*args)


def local(right_side, tiles, pattern, counts):
    nrhs, rows = right_side.shape
    bundles, slots, rays, cells = tiles.shape
    blocks = BLK_DEV // 2
    half = blocks * cells
    slots_in = (pattern.T, counts.T)

    def shape(columns, dtype=F32):
        return jax.ShapeDtypeStruct((nrhs, columns), dtype)

    def spread(value, axis):
        n = lax.axis_size(axis)
        moved = [
            lax.ppermute(value, axis, [(i, i ^ by) for i in range(n)]) for by in (1, 3, 2)
        ]
        return [value] + moved

    def swap(value):
        return lax.ppermute(value, "core", [(0, 1), (1, 0)])

    def over_cell(partial):
        own, left, right, far = lax.optimization_barrier(spread(partial, "x"))
        return spread((own + far) + (left + right), "y")

    halves = [shape(half + 128)] * 2
    store = [pltpu.VMEM((nrhs, 2 * (half + cells)), F32)]
    keep, send, tiles = call(
        first_adjoint, halves + [jax.ShapeDtypeStruct(tiles.shape, tiles.dtype)],
        [HBM] * 4,
        [pltpu.with_memory_space_constraint(z, pltpu.HBM) for z in (*slots_in, right_side, tiles)],
        store + [
            pltpu.SMEM((slots, bundles), jnp.int32), pltpu.SMEM((1, bundles), jnp.int32),
            pltpu.VMEM(right_side.shape, F32), pltpu.SemaphoreType.DMA((bundles + 3,)),
        ],
    )
    turned, = call(
        turn, [jax.ShapeDtypeStruct((bundles, slots, cells, rays), tiles.dtype)], [VMEM], (tiles,)
    )
    u = right_side
    owns, others, alphas, betas = [], [], [], []
    for step in range(ITERS):
        prev = (owns[-1], alphas[-1]) if step else (right_side, right_side)
        packed, = call(
            pack, [shape(half + 128, jnp.int16)], [VMEM] * 2, (keep, swap(send))
        )
        v, beta = call(
            functools.partial(cell_vector, step == 0), [shape(half), shape(128)], [VMEM] * 6,
            (*spread(packed, "z"), *prev),
        )
        other = swap(v)
        owns.append(v)
        others.append(other)
        betas.append(beta)
        products, = call(
            forward, [shape(rows + 128)], [SMEM] * 2 + [VMEM] * 3, (*slots_in, v, other, turned),
            [pltpu.VMEM((nrhs, 2 * half + cells), BF16)],
        )
        rows_in = over_cell(products)
        if step + 1 < ITERS:
            keep, send, u, alpha = call(
                next_adjoint, halves + [shape(rows), shape(128)], [SMEM] * 2 + [VMEM] * 7,
                (*slots_in, *rows_in, u, beta, tiles), store,
            )
        else:
            squares, alpha = call(
                last_norm, [shape(128), shape(128)], [VMEM] * 6, (*rows_in, u, beta)
            )
        alphas.append(alpha)
    so_far = call(
        gather_up, [shape(half)] * 4 + [shape(128)] * 2, [VMEM] * (4 * ITERS),
        (*owns, *others, *alphas, *betas),
    )
    x, misfit = call(
        finish, [shape(2 * half), jax.ShapeDtypeStruct((1, nrhs), F32)], [VMEM] * 10,
        (*spread(squares + swap(squares), "z"), *so_far),
    )
    return x, misfit.reshape(nrhs)


def solution(mesh):
    parts = Mesh(mesh.devices.reshape(4, 2, 4, 4), ("z", "core", "x", "y"))
    ray, cell = ("z", "core"), ("x", "y")
    in_specs = (P(None, ray), P(ray, cell, None, None), P(ray, cell), P(ray, cell))
    out_specs = (P(None, cell), P())
    return jax.shard_map(local, mesh=parts, in_specs=in_specs, out_specs=out_specs, check_vma=False)
```

```python
import functools

import jax
import jax.numpy as jnp
from jax import lax
from jax.experimental import pallas as pl
from jax.experimental.pallas import tpu as pltpu
from jax.sharding import Mesh, PartitionSpec as P

BLK_DEV = 32
ITERS = 4
EPS = 1e-06
TINY = 1e-30
DIGITS = 8192.0
CODES = 32000.0
F32 = jnp.float32
BF16 = jnp.bfloat16

VMEM = pl.BlockSpec(memory_space=pltpu.VMEM)
SMEM = pl.BlockSpec(memory_space=pltpu.SMEM)
HBM = pl.BlockSpec(memory_space=pltpu.HBM)


def lane_sum(x):
    return jnp.sum(x, axis=1, keepdims=True)


def fold_sq(x, width):
    total = None
    for at in range(0, x.shape[1], width):
        piece = x[:, at : at + width]
        total = piece * piece if total is None else total + piece * piece
    return total


def wide(x):
    return jnp.broadcast_to(x, (x.shape[0], 128))


def slots_of(pattern_ref, counts_ref, second, dead):
    blocks = BLK_DEV // 2
    core = lax.axis_index("core")

    def block_of(b, s):
        found = pattern_ref[s, b]
        within = found % blocks
        at = jnp.where(found // blocks == core, within, within + second)
        return jnp.where(s < counts_ref[0, b], at, dead)

    return block_of


def scatter_products(u, block_of, tiles_ref, keep_ref, send_ref, acc_ref, copies=None):
    bundles, slots, rays, cells = tiles_ref.shape
    half = keep_ref.shape[1] - 128
    acc_ref[...] = jnp.zeros_like(acc_ref)
    low = u.astype(BF16)
    for b in range(bundles):
        if copies:
            copies[b].wait()
        rows = low[:, b * rays : (b + 1) * rays]
        for s in range(slots):
            part = jnp.dot(rows, tiles_ref[b, s], preferred_element_type=F32)
            at = pl.multiple_of(block_of(b, s) * cells, cells)
            acc_ref[:, pl.ds(at, cells)] += part
    squares = fold_sq(u, 128)
    for out_ref, at in ((keep_ref, 0), (send_ref, half + cells)):
        out_ref[:, :half] = acc_ref[:, at : at + half]
        out_ref[:, half:] = squares


def first_adjoint(
    source_p_ref, source_c_ref, source_u_ref, source_ref, keep_ref, send_ref, tiles_ref, acc_ref,
    pattern_ref, counts_ref, u_ref, sem,
):
    bundles = source_ref.shape[0]
    small = ((source_p_ref, pattern_ref), (source_c_ref, counts_ref), (source_u_ref, u_ref))
    first = [
        pltpu.make_async_copy(source, target, sem.at[bundles + at])
        for at, (source, target) in enumerate(small)
    ]
    copies = [
        pltpu.make_async_copy(source_ref.at[b], tiles_ref.at[b], sem.at[b])
        for b in range(bundles)
    ]
    for copy in first + copies:
        copy.start()
    for copy in first:
        copy.wait()
    put = slots_of(pattern_ref, counts_ref, BLK_DEV // 2 + 1, BLK_DEV // 2)
    scatter_products(u_ref[...], put, tiles_ref, keep_ref, send_ref, acc_ref, copies)


def split(value, digits):
    power = jnp.floor(jnp.log2(value))
    return power, value * jnp.exp2(-power) * digits


def encode(body, squares, out_ref):
    width = body.shape[1]
    peak = jnp.maximum(jnp.max(jnp.abs(body), axis=1, keepdims=True), TINY)
    power, mantissa = split(peak, DIGITS)
    mantissa = jnp.floor(mantissa) + 1.0
    scale = mantissa * jnp.exp2(power) * (1.0 / DIGITS)
    norm_power, norm = split(jnp.maximum(squares, TINY), DIGITS)
    high = jnp.floor(norm)
    low = (norm - high) * DIGITS
    lane = lax.broadcasted_iota(jnp.int32, (body.shape[0], 128), 1)
    fields = jnp.zeros_like(lane).astype(F32)
    for at, field in enumerate((power, mantissa, norm_power, high, low)):
        fields = jnp.where(lane == at, field, fields)

    def code(x):
        return jnp.round(x).astype(jnp.int32).astype(jnp.int16)

    out_ref[:, :width] = code(body * (CODES / scale))
    out_ref[:, width:] = code(fields)


def decode(ref):
    width = ref.shape[1] - 128
    codes = ref[...].astype(jnp.int32).astype(F32)
    power, mantissa, norm_power, high, low = [codes[:, width + at : width + at + 1] for at in range(5)]
    scale = mantissa * jnp.exp2(power) * (1.0 / DIGITS)
    norm = (high + low * (1.0 / DIGITS)) * jnp.exp2(norm_power) * (1.0 / DIGITS)
    return codes[:, :width] * (scale * (1.0 / CODES)), norm


def decoded_sum(*refs):
    own, left, right, far = [decode(ref) for ref in refs]
    return [(own[at] + far[at]) + (left[at] + right[at]) for at in range(2)]


def pack(keep_ref, other_ref, out_ref):
    total = keep_ref[...] + other_ref[...]
    width = total.shape[1] - 128
    encode(total[:, :width], lane_sum(total[:, width:]), out_ref)


def relay(own_ref, left_ref, right_ref, far_ref, out_ref):
    body, squares = decoded_sum(own_ref, left_ref, right_ref, far_ref)
    encode(body, squares, out_ref)


def ray_vector(own_ref, left_ref, right_ref, far_ref, prev_ref, beta_ref):
    total, squares = decoded_sum(own_ref, left_ref, right_ref, far_ref)
    alpha = jnp.sqrt(squares + EPS)
    u = total / alpha - (alpha / beta_ref[:, :1]) * prev_ref[...]
    return u, alpha


def next_adjoint(
    pattern_ref, counts_ref, own_ref, left_ref, right_ref, far_ref, prev_ref, beta_ref, tiles_ref,
    keep_ref, send_ref, u_ref, alpha_ref, acc_ref,
):
    u, alpha = ray_vector(own_ref, left_ref, right_ref, far_ref, prev_ref, beta_ref)
    u_ref[...] = u
    alpha_ref[...] = wide(alpha)
    put = slots_of(pattern_ref, counts_ref, BLK_DEV // 2 + 1, BLK_DEV // 2)
    scatter_products(u, put, tiles_ref, keep_ref, send_ref, acc_ref)


def last_norm(
    own_ref, left_ref, right_ref, far_ref, prev_ref, beta_ref, out_ref, alpha_ref
):
    u, alpha = ray_vector(own_ref, left_ref, right_ref, far_ref, prev_ref, beta_ref)
    alpha_ref[...] = wide(alpha)
    out_ref[...] = fold_sq(u, 128)


def cell_vector(
    first, own_ref, left_ref, right_ref, far_ref, prev_ref, alpha_ref, v_ref, beta_ref
):
    total, squares = decoded_sum(own_ref, left_ref, right_ref, far_ref)
    beta = jnp.sqrt(squares + EPS)
    v = total / beta
    if not first:
        v = v - (beta / alpha_ref[:, :1]) * prev_ref[...]
    v_ref[...] = v
    beta_ref[...] = wide(beta)


def turn(tiles_ref, out_ref):
    for b in range(tiles_ref.shape[0]):
        for s in range(tiles_ref.shape[1]):
            out_ref[b, s] = tiles_ref[b, s].T


def forward(pattern_ref, counts_ref, own_ref, other_ref, tiles_ref, out_ref, low_ref, sum_ref):
    bundles, slots, cells, rays = tiles_ref.shape
    width = own_ref.shape[1]
    own, other = own_ref[...], other_ref[...]
    low_ref[:, :width] = own.astype(BF16)
    low_ref[:, width : 2 * width] = other.astype(BF16)
    low_ref[:, 2 * width :] = jnp.zeros((own.shape[0], cells), BF16)
    get = slots_of(pattern_ref, counts_ref, BLK_DEV // 2, BLK_DEV)
    for b in range(bundles):
        acc = None
        for s in range(slots):
            at = pl.multiple_of(get(b, s) * cells, cells)
            part = jnp.dot(
                low_ref[:, pl.ds(at, cells)], tiles_ref[b, s], preferred_element_type=F32
            )
            acc = part if acc is None else acc + part
        sum_ref[:, b * rays : (b + 1) * rays] = acc
    encode(sum_ref[...], lane_sum(fold_sq(own, 128) + fold_sq(other, 128)), out_ref)


def gather_up(*refs):
    count = ITERS
    own_refs, other_refs = refs[:count], refs[count : 2 * count]
    alpha_refs, beta_refs = refs[2 * count : 3 * count], refs[3 * count : 4 * count]
    x_refs, w_refs, phibar_ref, rhobar_ref = refs[4 * count : 4 * count + 2], refs[
        4 * count + 2 : 4 * count + 4], refs[-2], refs[-1]
    alphas = [ref[:, :1] for ref in alpha_refs]
    betas = [ref[:, :1] for ref in beta_refs]
    phibar, rhobar = betas[0], alphas[0]
    steps, turns = [], []
    for k in range(count - 1):
        beta = betas[k + 1]
        rho = jnp.sqrt(rhobar * rhobar + beta * beta)
        cosine, sine = rhobar / rho, beta / rho
        steps.append(cosine * phibar / rho)
        phibar = sine * phibar
        turns.append(sine * alphas[k + 1] / rho)
        rhobar = -cosine * alphas[k + 1]
    for refs, x_ref, w_ref in zip((own_refs, other_refs), x_refs, w_refs):
        w = refs[0][...] / alphas[0]
        x = steps[0] * w
        for k in range(1, count):
            w = refs[k][...] / alphas[k] - turns[k - 1] * w
            if k + 1 < count:
                x = x + steps[k] * w
        x_ref[...] = x
        w_ref[...] = w
    phibar_ref[...] = wide(phibar)
    rhobar_ref[...] = wide(rhobar)


def finish(
    own_ref, left_ref, right_ref, far_ref, own_x_ref, other_x_ref, own_w_ref,
    other_w_ref, phibar_ref, rhobar_ref, x_ref, misfit_ref,
):
    width = own_x_ref.shape[1]
    total = (own_ref[...] + far_ref[...]) + (left_ref[...] + right_ref[...])
    beta = jnp.sqrt(lane_sum(total) + EPS)
    phibar, rhobar = phibar_ref[:, :1], rhobar_ref[:, :1]
    rho = jnp.sqrt(rhobar * rhobar + beta * beta)
    step = (rhobar / rho) * phibar / rho
    core = lax.axis_index("core")
    for half, xs_ref, w_ref in ((core, own_x_ref, own_w_ref), (1 - core, other_x_ref, other_w_ref)):
        at = pl.multiple_of(half * width, width)
        x_ref[:, pl.ds(at, width)] = xs_ref[...] + step * w_ref[...]
    last = wide((beta / rho) * phibar)
    row = lax.broadcasted_iota(jnp.int32, last.shape, 0)
    lane = lax.broadcasted_iota(jnp.int32, last.shape, 1)
    across = jnp.sum(jnp.where(row == lane, last, 0.0), axis=0, keepdims=True)
    misfit_ref[...] = across[:, : misfit_ref.shape[1]]


def call(body, outs, specs, args, scratch=()):
    return pl.pallas_call(
        body,
        out_shape=outs,
        in_specs=specs,
        out_specs=[VMEM] * len(outs),
        scratch_shapes=list(scratch),
        compiler_params=pltpu.CompilerParams(vmem_limit_bytes=12 << 20),
    )(*args)


def local(right_side, tiles, pattern, counts):
    nrhs, rows = right_side.shape
    bundles, slots, rays, cells = tiles.shape
    blocks = BLK_DEV // 2
    half = blocks * cells
    slots_in = (pattern.T, counts.T)

    def shape(columns, dtype=F32):
        return jax.ShapeDtypeStruct((nrhs, columns), dtype)

    def spread(value, axis):
        n = lax.axis_size(axis)
        moved = [
            lax.ppermute(value, axis, [(i, i ^ by) for i in range(n)]) for by in (1, 3, 2)
        ]
        return [value] + moved

    def swap(value):
        return lax.ppermute(value, "core", [(0, 1), (1, 0)])

    def over_cell(partial):
        summed, = call(
            relay, [shape(rows + 128, jnp.int16)], [VMEM] * 4, spread(partial, "x")
        )
        return spread(summed, "y")

    halves = [shape(half + 128)] * 2
    store = [pltpu.VMEM((nrhs, 2 * (half + cells)), F32)]
    keep, send, tiles = call(
        first_adjoint, halves + [jax.ShapeDtypeStruct(tiles.shape, tiles.dtype)],
        [HBM] * 4,
        [pltpu.with_memory_space_constraint(z, pltpu.HBM) for z in (*slots_in, right_side, tiles)],
        store + [
            pltpu.SMEM((slots, bundles), jnp.int32), pltpu.SMEM((1, bundles), jnp.int32),
            pltpu.VMEM(right_side.shape, F32), pltpu.SemaphoreType.DMA((bundles + 3,)),
        ],
    )
    turned, = call(
        turn, [jax.ShapeDtypeStruct((bundles, slots, cells, rays), tiles.dtype)], [VMEM], (tiles,)
    )
    u = right_side
    owns, others, alphas, betas = [], [], [], []
    for step in range(ITERS):
        prev = (owns[-1], alphas[-1]) if step else (right_side, right_side)
        packed, = call(
            pack, [shape(half + 128, jnp.int16)], [VMEM] * 2, (keep, swap(send))
        )
        v, beta = call(
            functools.partial(cell_vector, step == 0), [shape(half), shape(128)], [VMEM] * 6,
            (*spread(packed, "z"), *prev),
        )
        other = swap(v)
        owns.append(v)
        others.append(other)
        betas.append(beta)
        products, = call(
            forward, [shape(rows + 128, jnp.int16)], [SMEM] * 2 + [VMEM] * 3, (*slots_in, v, other, turned),
            [pltpu.VMEM((nrhs, 2 * half + cells), BF16), pltpu.VMEM((nrhs, rows), F32)],
        )
        rows_in = over_cell(products)
        if step + 1 < ITERS:
            keep, send, u, alpha = call(
                next_adjoint, halves + [shape(rows), shape(128)], [SMEM] * 2 + [VMEM] * 7,
                (*slots_in, *rows_in, u, beta, tiles), store,
            )
        else:
            squares, alpha = call(
                last_norm, [shape(128), shape(128)], [VMEM] * 6, (*rows_in, u, beta)
            )
        alphas.append(alpha)
    so_far = call(
        gather_up, [shape(half)] * 4 + [shape(128)] * 2, [VMEM] * (4 * ITERS),
        (*owns, *others, *alphas, *betas),
    )
    x, misfit = call(
        finish, [shape(2 * half), jax.ShapeDtypeStruct((1, nrhs), F32)], [VMEM] * 10,
        (*spread(squares + swap(squares), "z"), *so_far),
    )
    return x, misfit.reshape(nrhs)


def solution(mesh):
    parts = Mesh(mesh.devices.reshape(4, 2, 4, 4), ("z", "core", "x", "y"))
    ray, cell = ("z", "core"), ("x", "y")
    in_specs = (P(None, ray), P(ray, cell, None, None), P(ray, cell), P(ray, cell))
    out_specs = (P(None, cell), P())
    return jax.shard_map(local, mesh=parts, in_specs=in_specs, out_specs=out_specs, check_vma=False)
```

```python
import functools

import jax
import jax.numpy as jnp
from jax import lax
from jax.experimental import pallas as pl
from jax.experimental.pallas import tpu as pltpu
from jax.sharding import Mesh, PartitionSpec as P

BLK_DEV = 32
GROUP = 8
ITERS = 4
EPS = 1e-06
TINY = 1e-30
DIGITS = 8192.0
CODES = 32000.0
F32 = jnp.float32
BF16 = jnp.bfloat16

VMEM = pl.BlockSpec(memory_space=pltpu.VMEM)
SMEM = pl.BlockSpec(memory_space=pltpu.SMEM)
HBM = pl.BlockSpec(memory_space=pltpu.HBM)


def lane_sum(x):
    return jnp.sum(x, axis=1, keepdims=True)


def fold_sq(x, width):
    total = None
    for at in range(0, x.shape[1], width):
        piece = x[:, at : at + width]
        total = piece * piece if total is None else total + piece * piece
    return total


def wide(x):
    return jnp.broadcast_to(x, (x.shape[0], 128))


def slots_of(pattern_ref, counts_ref, second, dead):
    blocks = BLK_DEV // 2
    core = lax.axis_index("core")

    def block_of(b, s):
        found = pattern_ref[s, b]
        within = found % blocks
        at = jnp.where(found // blocks == core, within, within + second)
        return jnp.where(s < counts_ref[0, b], at, dead)

    return block_of


def fill_lists(pattern_ref, counts_ref, lists_ref):
    slots, bundles = pattern_ref.shape
    most = slots * bundles
    blocks = BLK_DEV // 2
    core = lax.axis_index("core")
    for i in range(most):
        for at, value in ((0, 0), (most, blocks), (2 * most, 0), (3 * most, blocks)):
            lists_ref[at + i] = jnp.int32(value)
    lengths = [jnp.int32(0), jnp.int32(0)]
    for b in range(bundles):
        for s in range(slots):
            found = pattern_ref[s, b]
            mine = (found // blocks == core).astype(jnp.int32)
            live = (s < counts_ref[0, b]).astype(jnp.int32)
            at = jnp.where(mine == 1, 2 * most + lengths[1], lengths[0])
            at = jnp.where(live == 1, at, 4 * most + 2)
            lists_ref[at] = jnp.int32(b * slots + s)
            lists_ref[at + most] = found % blocks
            lengths = [lengths[0] + live * (1 - mine), lengths[1] + live * mine]
    lists_ref[4 * most] = lengths[0]
    lists_ref[4 * most + 1] = lengths[1]


def listed_products(lists_ref, mine, tiles_ref, one):
    most = tiles_ref.shape[0]
    base = 2 * most if mine else 0

    def group(g, carry):
        for i in range(GROUP):
            at = base + g * GROUP + i
            one(lists_ref[at], lists_ref[at + most])
        return carry

    length = lists_ref[4 * most + (1 if mine else 0)]
    lax.fori_loop(0, (length + GROUP - 1) // GROUP, group, 0)


def half_adjoint(lists_ref, mine, u, tiles_ref, out_ref, acc_ref, low_ref, slots):
    cells = tiles_ref.shape[2]
    rays = tiles_ref.shape[1]
    half = out_ref.shape[1] - 128
    acc_ref[...] = jnp.zeros_like(acc_ref)
    low_ref[...] = u.astype(BF16)

    def one(tile, block):
        rows = low_ref[:, pl.ds(pl.multiple_of(tile // slots * rays, rays), rays)]
        part = jnp.dot(rows, tiles_ref[tile], preferred_element_type=F32)
        acc_ref[:, pl.ds(pl.multiple_of(block * cells, cells), cells)] += part

    listed_products(lists_ref, mine, tiles_ref, one)
    out_ref[:, :half] = acc_ref[:, :half]
    out_ref[:, half:] = fold_sq(u, 128)


def half_forward(lists_ref, mine, v, tiles_ref, sum_ref, low_ref, slots):
    cells, rays = tiles_ref.shape[1:]
    half = v.shape[1]
    low_ref[:, :half] = v.astype(BF16)
    low_ref[:, half:] = jnp.zeros((v.shape[0], cells), BF16)

    def one(tile, block):
        rows = low_ref[:, pl.ds(pl.multiple_of(block * cells, cells), cells)]
        part = jnp.dot(rows, tiles_ref[tile], preferred_element_type=F32)
        sum_ref[:, pl.ds(pl.multiple_of(tile // slots * rays, rays), rays)] += part

    listed_products(lists_ref, mine, tiles_ref, one)


def scatter_products(u, block_of, tiles_ref, keep_ref, send_ref, acc_ref, copies=None):
    bundles, slots, rays, cells = tiles_ref.shape
    half = keep_ref.shape[1] - 128
    acc_ref[...] = jnp.zeros_like(acc_ref)
    low = u.astype(BF16)
    for b in range(bundles):
        if copies:
            copies[b].wait()
        rows = low[:, b * rays : (b + 1) * rays]
        for s in range(slots):
            part = jnp.dot(rows, tiles_ref[b, s], preferred_element_type=F32)
            at = pl.multiple_of(block_of(b, s) * cells, cells)
            acc_ref[:, pl.ds(at, cells)] += part
    squares = fold_sq(u, 128)
    for out_ref, at in ((keep_ref, 0), (send_ref, half + cells)):
        out_ref[:, :half] = acc_ref[:, at : at + half]
        out_ref[:, half:] = squares


def first_adjoint(
    source_p_ref, source_c_ref, source_u_ref, source_ref, keep_ref, send_ref, tiles_ref, lists_ref,
    acc_ref, pattern_ref, counts_ref, u_ref, sem,
):
    bundles = source_ref.shape[0]
    small = ((source_p_ref, pattern_ref), (source_c_ref, counts_ref), (source_u_ref, u_ref))
    first = [
        pltpu.make_async_copy(source, target, sem.at[bundles + at])
        for at, (source, target) in enumerate(small)
    ]
    copies = [
        pltpu.make_async_copy(source_ref.at[b], tiles_ref.at[b], sem.at[b])
        for b in range(bundles)
    ]
    for copy in first + copies:
        copy.start()
    for copy in first:
        copy.wait()
    fill_lists(pattern_ref, counts_ref, lists_ref)
    put = slots_of(pattern_ref, counts_ref, BLK_DEV // 2 + 1, BLK_DEV // 2)
    scatter_products(u_ref[...], put, tiles_ref, keep_ref, send_ref, acc_ref, copies)


def split(value, digits):
    power = jnp.floor(jnp.log2(value))
    return power, value * jnp.exp2(-power) * digits


def encode(body, squares, out_ref):
    width = body.shape[1]
    peak = jnp.maximum(jnp.max(jnp.abs(body), axis=1, keepdims=True), TINY)
    power, mantissa = split(peak, DIGITS)
    mantissa = jnp.floor(mantissa) + 1.0
    scale = mantissa * jnp.exp2(power) * (1.0 / DIGITS)
    norm_power, norm = split(jnp.maximum(squares, TINY), DIGITS)
    high = jnp.floor(norm)
    low = (norm - high) * DIGITS
    lane = lax.broadcasted_iota(jnp.int32, (body.shape[0], 128), 1)
    fields = jnp.zeros_like(lane).astype(F32)
    for at, field in enumerate((power, mantissa, norm_power, high, low)):
        fields = jnp.where(lane == at, field, fields)

    def code(x):
        return jnp.round(x).astype(jnp.int32).astype(jnp.int16)

    out_ref[:, :width] = code(body * (CODES / scale))
    out_ref[:, width:] = code(fields)


def decode(ref):
    width = ref.shape[1] - 128
    codes = ref[...].astype(jnp.int32).astype(F32)
    power, mantissa, norm_power, high, low = [codes[:, width + at : width + at + 1] for at in range(5)]
    scale = mantissa * jnp.exp2(power) * (1.0 / DIGITS)
    norm = (high + low * (1.0 / DIGITS)) * jnp.exp2(norm_power) * (1.0 / DIGITS)
    return codes[:, :width] * (scale * (1.0 / CODES)), norm


def decoded_sum(*refs):
    own, left, right, far = [decode(ref) for ref in refs]
    return [(own[at] + far[at]) + (left[at] + right[at]) for at in range(2)]


def pack(keep_ref, other_ref, out_ref):
    total = keep_ref[...] + other_ref[...]
    width = total.shape[1] - 128
    encode(total[:, :width], lane_sum(total[:, width:]), out_ref)


def relay(own_ref, left_ref, right_ref, far_ref, out_ref):
    body, squares = decoded_sum(own_ref, left_ref, right_ref, far_ref)
    encode(body, squares, out_ref)


def ray_vector(own_ref, left_ref, right_ref, far_ref, prev_ref, beta_ref):
    total, squares = decoded_sum(own_ref, left_ref, right_ref, far_ref)
    alpha = jnp.sqrt(squares + EPS)
    u = total / alpha - (alpha / beta_ref[:, :1]) * prev_ref[...]
    return u, alpha


def adjoint_send(
    slots, lists_ref, own_ref, left_ref, right_ref, far_ref, prev_ref, beta_ref, tiles_ref,
    send_ref, u_ref, alpha_ref, acc_ref, low_ref,
):
    u, alpha = ray_vector(own_ref, left_ref, right_ref, far_ref, prev_ref, beta_ref)
    u_ref[...] = u
    alpha_ref[...] = wide(alpha)
    half_adjoint(lists_ref, False, u, tiles_ref, send_ref, acc_ref, low_ref, slots)


def adjoint_keep(slots, lists_ref, u_ref, tiles_ref, keep_ref, acc_ref, low_ref):
    half_adjoint(lists_ref, True, u_ref[...], tiles_ref, keep_ref, acc_ref, low_ref, slots)


def last_norm(
    own_ref, left_ref, right_ref, far_ref, prev_ref, beta_ref, out_ref, alpha_ref
):
    u, alpha = ray_vector(own_ref, left_ref, right_ref, far_ref, prev_ref, beta_ref)
    alpha_ref[...] = wide(alpha)
    out_ref[...] = fold_sq(u, 128)


def cell_vector(
    first, own_ref, left_ref, right_ref, far_ref, prev_ref, alpha_ref, v_ref, beta_ref
):
    total, squares = decoded_sum(own_ref, left_ref, right_ref, far_ref)
    beta = jnp.sqrt(squares + EPS)
    v = total / beta
    if not first:
        v = v - (beta / alpha_ref[:, :1]) * prev_ref[...]
    v_ref[...] = v
    beta_ref[...] = wide(beta)


def turn(tiles_ref, out_ref):
    for tile in range(tiles_ref.shape[0]):
        out_ref[tile] = tiles_ref[tile].T


def forward_own(slots, lists_ref, own_ref, tiles_ref, part_ref, low_ref):
    part_ref[...] = jnp.zeros_like(part_ref)
    own = own_ref[...]
    half_forward(lists_ref, True, own, tiles_ref, part_ref, low_ref, slots)
    part_ref[:, part_ref.shape[1] - 128 :] = fold_sq(own, 128)


def forward_other(slots, lists_ref, part_ref, other_ref, tiles_ref, out_ref, sum_ref, low_ref):
    width = sum_ref.shape[1]
    sum_ref[...] = part_ref[:, :width]
    other = other_ref[...]
    half_forward(lists_ref, False, other, tiles_ref, sum_ref, low_ref, slots)
    encode(sum_ref[...], lane_sum(part_ref[:, width:] + fold_sq(other, 128)), out_ref)


def gather_up(*refs):
    count = ITERS
    own_refs, other_refs = refs[:count], refs[count : 2 * count]
    alpha_refs, beta_refs = refs[2 * count : 3 * count], refs[3 * count : 4 * count]
    x_refs, w_refs, phibar_ref, rhobar_ref = refs[4 * count : 4 * count + 2], refs[
        4 * count + 2 : 4 * count + 4], refs[-2], refs[-1]
    alphas = [ref[:, :1] for ref in alpha_refs]
    betas = [ref[:, :1] for ref in beta_refs]
    phibar, rhobar = betas[0], alphas[0]
    steps, turns = [], []
    for k in range(count - 1):
        beta = betas[k + 1]
        rho = jnp.sqrt(rhobar * rhobar + beta * beta)
        cosine, sine = rhobar / rho, beta / rho
        steps.append(cosine * phibar / rho)
        phibar = sine * phibar
        turns.append(sine * alphas[k + 1] / rho)
        rhobar = -cosine * alphas[k + 1]
    for refs, x_ref, w_ref in zip((own_refs, other_refs), x_refs, w_refs):
        w = refs[0][...] / alphas[0]
        x = steps[0] * w
        for k in range(1, count):
            w = refs[k][...] / alphas[k] - turns[k - 1] * w
            if k + 1 < count:
                x = x + steps[k] * w
        x_ref[...] = x
        w_ref[...] = w
    phibar_ref[...] = wide(phibar)
    rhobar_ref[...] = wide(rhobar)


def finish(
    own_ref, left_ref, right_ref, far_ref, own_x_ref, other_x_ref, own_w_ref,
    other_w_ref, phibar_ref, rhobar_ref, x_ref, misfit_ref,
):
    width = own_x_ref.shape[1]
    total = (own_ref[...] + far_ref[...]) + (left_ref[...] + right_ref[...])
    beta = jnp.sqrt(lane_sum(total) + EPS)
    phibar, rhobar = phibar_ref[:, :1], rhobar_ref[:, :1]
    rho = jnp.sqrt(rhobar * rhobar + beta * beta)
    step = (rhobar / rho) * phibar / rho
    core = lax.axis_index("core")
    for half, xs_ref, w_ref in ((core, own_x_ref, own_w_ref), (1 - core, other_x_ref, other_w_ref)):
        at = pl.multiple_of(half * width, width)
        x_ref[:, pl.ds(at, width)] = xs_ref[...] + step * w_ref[...]
    last = wide((beta / rho) * phibar)
    row = lax.broadcasted_iota(jnp.int32, last.shape, 0)
    lane = lax.broadcasted_iota(jnp.int32, last.shape, 1)
    across = jnp.sum(jnp.where(row == lane, last, 0.0), axis=0, keepdims=True)
    misfit_ref[...] = across[:, : misfit_ref.shape[1]]


def call(body, outs, specs, args, scratch=(), out_specs=None):
    return pl.pallas_call(
        body,
        out_shape=outs,
        in_specs=specs,
        out_specs=out_specs or [VMEM] * len(outs),
        scratch_shapes=list(scratch),
        compiler_params=pltpu.CompilerParams(vmem_limit_bytes=12 << 20),
    )(*args)


def local(right_side, tiles, pattern, counts):
    nrhs, rows = right_side.shape
    bundles, slots, rays, cells = tiles.shape
    blocks = BLK_DEV // 2
    half = blocks * cells
    most = bundles * slots
    slots_in = (pattern.T, counts.T)

    def shape(columns, dtype=F32):
        return jax.ShapeDtypeStruct((nrhs, columns), dtype)

    def spread(value, axis):
        n = lax.axis_size(axis)
        moved = [
            lax.ppermute(value, axis, [(i, i ^ by) for i in range(n)]) for by in (1, 3, 2)
        ]
        return [value] + moved

    def swap(value):
        return lax.ppermute(value, "core", [(0, 1), (1, 0)])

    def over_cell(partial):
        summed, = call(
            relay, [shape(rows + 128, jnp.int16)], [VMEM] * 4, spread(partial, "x")
        )
        return spread(summed, "y")

    halves = [shape(half + 128)] * 2
    keep, send, tiles, lists = call(
        first_adjoint,
        halves + [
            jax.ShapeDtypeStruct(tiles.shape, tiles.dtype),
            jax.ShapeDtypeStruct((4 * most + 3 + most,), jnp.int32),
        ],
        [HBM] * 4,
        [pltpu.with_memory_space_constraint(z, pltpu.HBM) for z in (*slots_in, right_side, tiles)],
        [
            pltpu.VMEM((nrhs, 2 * (half + cells)), F32),
            pltpu.SMEM((slots, bundles), jnp.int32), pltpu.SMEM((1, bundles), jnp.int32),
            pltpu.VMEM(right_side.shape, F32), pltpu.SemaphoreType.DMA((bundles + 3,)),
        ],
        [VMEM] * 3 + [SMEM],
    )
    tiles = tiles.reshape(most, rays, cells)
    turned, = call(turn, [jax.ShapeDtypeStruct((most, cells, rays), tiles.dtype)], [VMEM], (tiles,))
    adjoint_scratch = [pltpu.VMEM((nrhs, half + cells), F32), pltpu.VMEM((nrhs, rows), BF16)]
    low = pltpu.VMEM((nrhs, half + cells), BF16)
    u = right_side
    owns, others, alphas, betas = [], [], [], []
    for step in range(ITERS):
        prev = (owns[-1], alphas[-1]) if step else (right_side, right_side)
        packed, = call(
            pack, [shape(half + 128, jnp.int16)], [VMEM] * 2, (keep, swap(send))
        )
        v, beta = call(
            functools.partial(cell_vector, step == 0), [shape(half), shape(128)], [VMEM] * 6,
            (*spread(packed, "z"), *prev),
        )
        other = swap(v)
        owns.append(v)
        others.append(other)
        betas.append(beta)
        part, = call(
            functools.partial(forward_own, slots), [shape(rows + 128)], [SMEM] + [VMEM] * 2,
            (lists, v, turned), [low],
        )
        products, = call(
            functools.partial(forward_other, slots), [shape(rows + 128, jnp.int16)],
            [SMEM] + [VMEM] * 3, (lists, part, other, turned), [pltpu.VMEM((nrhs, rows), F32), low],
        )
        rows_in = over_cell(products)
        if step + 1 < ITERS:
            send, u, alpha = call(
                functools.partial(adjoint_send, slots),
                [shape(half + 128), shape(rows), shape(128)], [SMEM] + [VMEM] * 7,
                (lists, *rows_in, u, beta, tiles), adjoint_scratch,
            )
            keep, = call(
                functools.partial(adjoint_keep, slots), [shape(half + 128)],
                [SMEM] + [VMEM] * 2, (lists, u, tiles), adjoint_scratch,
            )
        else:
            squares, alpha = call(
                last_norm, [shape(128), shape(128)], [VMEM] * 6, (*rows_in, u, beta)
            )
        alphas.append(alpha)
    so_far = call(
        gather_up, [shape(half)] * 4 + [shape(128)] * 2, [VMEM] * (4 * ITERS),
        (*owns, *others, *alphas, *betas),
    )
    x, misfit = call(
        finish, [shape(2 * half), jax.ShapeDtypeStruct((1, nrhs), F32)], [VMEM] * 10,
        (*spread(squares + swap(squares), "z"), *so_far),
    )
    return x, misfit.reshape(nrhs)


def solution(mesh):
    parts = Mesh(mesh.devices.reshape(4, 2, 4, 4), ("z", "core", "x", "y"))
    ray, cell = ("z", "core"), ("x", "y")
    in_specs = (P(None, ray), P(ray, cell, None, None), P(ray, cell), P(ray, cell))
    out_specs = (P(None, cell), P())
    return jax.shard_map(local, mesh=parts, in_specs=in_specs, out_specs=out_specs, check_vma=False)
```

```python
import functools

import jax
import jax.numpy as jnp
from jax import lax
from jax.experimental import pallas as pl
from jax.experimental.pallas import tpu as pltpu
from jax.sharding import Mesh, PartitionSpec as P

BLK_DEV = 32
HEAD = 20
GROUP = 4
ITERS = 4
EPS = 1e-06
TINY = 1e-30
DIGITS = 8192.0
CODES = 32000.0
F32 = jnp.float32
BF16 = jnp.bfloat16

VMEM = pl.BlockSpec(memory_space=pltpu.VMEM)
SMEM = pl.BlockSpec(memory_space=pltpu.SMEM)
HBM = pl.BlockSpec(memory_space=pltpu.HBM)


def lane_sum(x):
    return jnp.sum(x, axis=1, keepdims=True)


def fold_sq(x, width):
    total = None
    for at in range(0, x.shape[1], width):
        piece = x[:, at : at + width]
        total = piece * piece if total is None else total + piece * piece
    return total


def wide(x):
    return jnp.broadcast_to(x, (x.shape[0], 128))


def slots_of(pattern_ref, counts_ref, second, dead):
    blocks = BLK_DEV // 2
    core = lax.axis_index("core")

    def block_of(b, s):
        found = pattern_ref[s, b]
        within = found % blocks
        at = jnp.where(found // blocks == core, within, within + second)
        return jnp.where(s < counts_ref[0, b], at, dead)

    return block_of


def fill_lists(pattern_ref, counts_ref, lists_ref):
    slots, bundles = pattern_ref.shape
    most = slots * bundles
    blocks = BLK_DEV // 2
    core = lax.axis_index("core")
    for i in range(most):
        for at, value in ((0, 0), (most, blocks), (2 * most, 0), (3 * most, blocks)):
            lists_ref[at + i] = jnp.int32(value)
    lengths = [jnp.int32(0), jnp.int32(0)]
    for b in range(bundles):
        for s in range(slots):
            found = pattern_ref[s, b]
            mine = (found // blocks == core).astype(jnp.int32)
            live = (s < counts_ref[0, b]).astype(jnp.int32)
            at = jnp.where(mine == 1, 2 * most + lengths[1], lengths[0])
            at = jnp.where(live == 1, at, 4 * most + 2)
            lists_ref[at] = jnp.int32(b * slots + s)
            lists_ref[at + most] = found % blocks
            lengths = [lengths[0] + live * (1 - mine), lengths[1] + live * mine]
    lists_ref[4 * most] = lengths[0]
    lists_ref[4 * most + 1] = lengths[1]


def listed_products(lists_ref, mine, tiles_ref, one):
    most = tiles_ref.shape[0]
    base = 2 * most if mine else 0

    def run(first, count):
        for i in range(count):
            one(lists_ref[first + i], lists_ref[first + i + most])

    def group(g, carry):
        run(base + HEAD + g * GROUP, GROUP)
        return carry

    run(base, min(HEAD, most))
    if HEAD < most:
        rest = jnp.maximum(lists_ref[4 * most + (1 if mine else 0)] - HEAD, 0)
        lax.fori_loop(0, (rest + GROUP - 1) // GROUP, group, 0)


def half_adjoint(lists_ref, mine, u, tiles_ref, out_ref, acc_ref, low_ref, slots):
    cells = tiles_ref.shape[2]
    rays = tiles_ref.shape[1]
    half = out_ref.shape[1] - 128
    acc_ref[...] = jnp.zeros_like(acc_ref)
    low_ref[...] = u.astype(BF16)

    def one(tile, block):
        rows = low_ref[:, pl.ds(pl.multiple_of(tile // slots * rays, rays), rays)]
        part = jnp.dot(rows, tiles_ref[tile], preferred_element_type=F32)
        acc_ref[:, pl.ds(pl.multiple_of(block * cells, cells), cells)] += part

    listed_products(lists_ref, mine, tiles_ref, one)
    out_ref[:, :half] = acc_ref[:, :half]
    out_ref[:, half:] = fold_sq(u, 128)


def half_forward(lists_ref, mine, v, tiles_ref, sum_ref, low_ref, slots):
    cells, rays = tiles_ref.shape[1:]
    half = v.shape[1]
    low_ref[:, :half] = v.astype(BF16)
    low_ref[:, half:] = jnp.zeros((v.shape[0], cells), BF16)

    def one(tile, block):
        rows = low_ref[:, pl.ds(pl.multiple_of(block * cells, cells), cells)]
        part = jnp.dot(rows, tiles_ref[tile], preferred_element_type=F32)
        sum_ref[:, pl.ds(pl.multiple_of(tile // slots * rays, rays), rays)] += part

    listed_products(lists_ref, mine, tiles_ref, one)


def scatter_products(u, block_of, tiles_ref, keep_ref, send_ref, acc_ref, copies=None):
    bundles, slots, rays, cells = tiles_ref.shape
    half = keep_ref.shape[1] - 128
    acc_ref[...] = jnp.zeros_like(acc_ref)
    low = u.astype(BF16)
    for b in range(bundles):
        if copies:
            copies[b].wait()
        rows = low[:, b * rays : (b + 1) * rays]
        for s in range(slots):
            part = jnp.dot(rows, tiles_ref[b, s], preferred_element_type=F32)
            at = pl.multiple_of(block_of(b, s) * cells, cells)
            acc_ref[:, pl.ds(at, cells)] += part
    squares = fold_sq(u, 128)
    for out_ref, at in ((keep_ref, 0), (send_ref, half + cells)):
        out_ref[:, :half] = acc_ref[:, at : at + half]
        out_ref[:, half:] = squares


def first_adjoint(
    source_p_ref, source_c_ref, source_u_ref, source_ref, keep_ref, send_ref, tiles_ref, acc_ref,
    pattern_ref, counts_ref, u_ref, sem,
):
    bundles = source_ref.shape[0]
    small = ((source_p_ref, pattern_ref), (source_c_ref, counts_ref), (source_u_ref, u_ref))
    first = [
        pltpu.make_async_copy(source, target, sem.at[bundles + at])
        for at, (source, target) in enumerate(small)
    ]
    copies = [
        pltpu.make_async_copy(source_ref.at[b], tiles_ref.at[b], sem.at[b])
        for b in range(bundles)
    ]
    for copy in first + copies:
        copy.start()
    for copy in first:
        copy.wait()
    put = slots_of(pattern_ref, counts_ref, BLK_DEV // 2 + 1, BLK_DEV // 2)
    scatter_products(u_ref[...], put, tiles_ref, keep_ref, send_ref, acc_ref, copies)


def split(value, digits):
    power = jnp.floor(jnp.log2(value))
    return power, value * jnp.exp2(-power) * digits


def encode(body, squares, out_ref):
    width = body.shape[1]
    peak = jnp.maximum(jnp.max(jnp.abs(body), axis=1, keepdims=True), TINY)
    power, mantissa = split(peak, DIGITS)
    mantissa = jnp.floor(mantissa) + 1.0
    scale = mantissa * jnp.exp2(power) * (1.0 / DIGITS)
    norm_power, norm = split(jnp.maximum(squares, TINY), DIGITS)
    high = jnp.floor(norm)
    low = (norm - high) * DIGITS
    lane = lax.broadcasted_iota(jnp.int32, (body.shape[0], 128), 1)
    fields = jnp.zeros_like(lane).astype(F32)
    for at, field in enumerate((power, mantissa, norm_power, high, low)):
        fields = jnp.where(lane == at, field, fields)

    def code(x):
        return jnp.round(x).astype(jnp.int32).astype(jnp.int16)

    out_ref[:, :width] = code(body * (CODES / scale))
    out_ref[:, width:] = code(fields)


def decode(ref):
    width = ref.shape[1] - 128
    codes = ref[...].astype(jnp.int32).astype(F32)
    power, mantissa, norm_power, high, low = [codes[:, width + at : width + at + 1] for at in range(5)]
    scale = mantissa * jnp.exp2(power) * (1.0 / DIGITS)
    norm = (high + low * (1.0 / DIGITS)) * jnp.exp2(norm_power) * (1.0 / DIGITS)
    return codes[:, :width] * (scale * (1.0 / CODES)), norm


def decoded_sum(*refs):
    own, left, right, far = [decode(ref) for ref in refs]
    return [(own[at] + far[at]) + (left[at] + right[at]) for at in range(2)]


def pack(keep_ref, other_ref, out_ref):
    total = keep_ref[...] + other_ref[...]
    width = total.shape[1] - 128
    encode(total[:, :width], lane_sum(total[:, width:]), out_ref)


def relay(own_ref, left_ref, right_ref, far_ref, out_ref):
    body, squares = decoded_sum(own_ref, left_ref, right_ref, far_ref)
    encode(body, squares, out_ref)


def ray_vector(own_ref, left_ref, right_ref, far_ref, prev_ref, beta_ref):
    total, squares = decoded_sum(own_ref, left_ref, right_ref, far_ref)
    alpha = jnp.sqrt(squares + EPS)
    u = total / alpha - (alpha / beta_ref[:, :1]) * prev_ref[...]
    return u, alpha


def adjoint_send(
    slots, lists_ref, own_ref, left_ref, right_ref, far_ref, prev_ref, beta_ref, tiles_ref,
    send_ref, u_ref, alpha_ref, acc_ref, low_ref,
):
    u, alpha = ray_vector(own_ref, left_ref, right_ref, far_ref, prev_ref, beta_ref)
    u_ref[...] = u
    alpha_ref[...] = wide(alpha)
    half_adjoint(lists_ref, False, u, tiles_ref, send_ref, acc_ref, low_ref, slots)


def adjoint_keep(slots, lists_ref, u_ref, tiles_ref, keep_ref, acc_ref, low_ref):
    half_adjoint(lists_ref, True, u_ref[...], tiles_ref, keep_ref, acc_ref, low_ref, slots)


def last_norm(
    own_ref, left_ref, right_ref, far_ref, prev_ref, beta_ref, out_ref, alpha_ref
):
    u, alpha = ray_vector(own_ref, left_ref, right_ref, far_ref, prev_ref, beta_ref)
    alpha_ref[...] = wide(alpha)
    out_ref[...] = fold_sq(u, 128)


def cell_vector(
    first, own_ref, left_ref, right_ref, far_ref, prev_ref, alpha_ref, v_ref, beta_ref
):
    total, squares = decoded_sum(own_ref, left_ref, right_ref, far_ref)
    beta = jnp.sqrt(squares + EPS)
    v = total / beta
    if not first:
        v = v - (beta / alpha_ref[:, :1]) * prev_ref[...]
    v_ref[...] = v
    beta_ref[...] = wide(beta)


def turn(pattern_ref, counts_ref, tiles_ref, out_ref, lists_ref):
    fill_lists(pattern_ref, counts_ref, lists_ref)
    for tile in range(tiles_ref.shape[0]):
        out_ref[tile] = tiles_ref[tile].T


def forward_own(slots, lists_ref, own_ref, tiles_ref, part_ref, low_ref):
    part_ref[...] = jnp.zeros_like(part_ref)
    own = own_ref[...]
    half_forward(lists_ref, True, own, tiles_ref, part_ref, low_ref, slots)
    part_ref[:, part_ref.shape[1] - 128 :] = fold_sq(own, 128)


def forward_other(slots, lists_ref, part_ref, other_ref, tiles_ref, out_ref, sum_ref, low_ref):
    width = sum_ref.shape[1]
    sum_ref[...] = part_ref[:, :width]
    other = other_ref[...]
    half_forward(lists_ref, False, other, tiles_ref, sum_ref, low_ref, slots)
    encode(sum_ref[...], lane_sum(part_ref[:, width:] + fold_sq(other, 128)), out_ref)


def gather_up(*refs):
    count = ITERS
    own_refs, other_refs = refs[:count], refs[count : 2 * count]
    alpha_refs, beta_refs = refs[2 * count : 3 * count], refs[3 * count : 4 * count]
    x_refs, w_refs, phibar_ref, rhobar_ref = refs[4 * count : 4 * count + 2], refs[
        4 * count + 2 : 4 * count + 4], refs[-2], refs[-1]
    alphas = [ref[:, :1] for ref in alpha_refs]
    betas = [ref[:, :1] for ref in beta_refs]
    phibar, rhobar = betas[0], alphas[0]
    steps, turns = [], []
    for k in range(count - 1):
        beta = betas[k + 1]
        rho = jnp.sqrt(rhobar * rhobar + beta * beta)
        cosine, sine = rhobar / rho, beta / rho
        steps.append(cosine * phibar / rho)
        phibar = sine * phibar
        turns.append(sine * alphas[k + 1] / rho)
        rhobar = -cosine * alphas[k + 1]
    for refs, x_ref, w_ref in zip((own_refs, other_refs), x_refs, w_refs):
        w = refs[0][...] / alphas[0]
        x = steps[0] * w
        for k in range(1, count):
            w = refs[k][...] / alphas[k] - turns[k - 1] * w
            if k + 1 < count:
                x = x + steps[k] * w
        x_ref[...] = x
        w_ref[...] = w
    phibar_ref[...] = wide(phibar)
    rhobar_ref[...] = wide(rhobar)


def finish(
    own_ref, left_ref, right_ref, far_ref, own_x_ref, other_x_ref, own_w_ref,
    other_w_ref, phibar_ref, rhobar_ref, x_ref, misfit_ref,
):
    width = own_x_ref.shape[1]
    total = (own_ref[...] + far_ref[...]) + (left_ref[...] + right_ref[...])
    beta = jnp.sqrt(lane_sum(total) + EPS)
    phibar, rhobar = phibar_ref[:, :1], rhobar_ref[:, :1]
    rho = jnp.sqrt(rhobar * rhobar + beta * beta)
    step = (rhobar / rho) * phibar / rho
    core = lax.axis_index("core")
    for half, xs_ref, w_ref in ((core, own_x_ref, own_w_ref), (1 - core, other_x_ref, other_w_ref)):
        at = pl.multiple_of(half * width, width)
        x_ref[:, pl.ds(at, width)] = xs_ref[...] + step * w_ref[...]
    last = wide((beta / rho) * phibar)
    row = lax.broadcasted_iota(jnp.int32, last.shape, 0)
    lane = lax.broadcasted_iota(jnp.int32, last.shape, 1)
    across = jnp.sum(jnp.where(row == lane, last, 0.0), axis=0, keepdims=True)
    misfit_ref[...] = across[:, : misfit_ref.shape[1]]


def call(body, outs, specs, args, scratch=(), out_specs=None):
    return pl.pallas_call(
        body,
        out_shape=outs,
        in_specs=specs,
        out_specs=out_specs or [VMEM] * len(outs),
        scratch_shapes=list(scratch),
        compiler_params=pltpu.CompilerParams(vmem_limit_bytes=12 << 20),
    )(*args)


def local(right_side, tiles, pattern, counts):
    nrhs, rows = right_side.shape
    bundles, slots, rays, cells = tiles.shape
    blocks = BLK_DEV // 2
    half = blocks * cells
    most = bundles * slots
    slots_in = (pattern.T, counts.T)

    def shape(columns, dtype=F32):
        return jax.ShapeDtypeStruct((nrhs, columns), dtype)

    def spread(value, axis):
        n = lax.axis_size(axis)
        moved = [
            lax.ppermute(value, axis, [(i, i ^ by) for i in range(n)]) for by in (1, 3, 2)
        ]
        return [value] + moved

    def swap(value):
        return lax.ppermute(value, "core", [(0, 1), (1, 0)])

    def over_cell(partial):
        summed, = call(
            relay, [shape(rows + 128, jnp.int16)], [VMEM] * 4, spread(partial, "x")
        )
        return spread(summed, "y")

    halves = [shape(half + 128)] * 2
    keep, send, tiles = call(
        first_adjoint, halves + [jax.ShapeDtypeStruct(tiles.shape, tiles.dtype)],
        [HBM] * 4,
        [pltpu.with_memory_space_constraint(z, pltpu.HBM) for z in (*slots_in, right_side, tiles)],
        [
            pltpu.VMEM((nrhs, 2 * (half + cells)), F32),
            pltpu.SMEM((slots, bundles), jnp.int32), pltpu.SMEM((1, bundles), jnp.int32),
            pltpu.VMEM(right_side.shape, F32), pltpu.SemaphoreType.DMA((bundles + 3,)),
        ],
    )
    tiles = tiles.reshape(most, rays, cells)
    turned, lists = call(
        turn,
        [
            jax.ShapeDtypeStruct((most, cells, rays), tiles.dtype),
            jax.ShapeDtypeStruct((5 * most + 3,), jnp.int32),
        ],
        [SMEM] * 2 + [VMEM], (*slots_in, tiles), (), [VMEM, SMEM],
    )
    adjoint_scratch = [pltpu.VMEM((nrhs, half + cells), F32), pltpu.VMEM((nrhs, rows), BF16)]
    low = pltpu.VMEM((nrhs, half + cells), BF16)
    u = right_side
    owns, others, alphas, betas = [], [], [], []
    for step in range(ITERS):
        prev = (owns[-1], alphas[-1]) if step else (right_side, right_side)
        packed, = call(
            pack, [shape(half + 128, jnp.int16)], [VMEM] * 2, (keep, swap(send))
        )
        moved = spread(packed, "z")
        if step == 0:
            moved, turned, lists = lax.optimization_barrier((moved, turned, lists))
        v, beta = call(
            functools.partial(cell_vector, step == 0), [shape(half), shape(128)], [VMEM] * 6,
            (*moved, *prev),
        )
        other = swap(v)
        owns.append(v)
        others.append(other)
        betas.append(beta)
        part, = call(
            functools.partial(forward_own, slots), [shape(rows + 128)], [SMEM] + [VMEM] * 2,
            (lists, v, turned), [low],
        )
        products, = call(
            functools.partial(forward_other, slots), [shape(rows + 128, jnp.int16)],
            [SMEM] + [VMEM] * 3, (lists, part, other, turned), [pltpu.VMEM((nrhs, rows), F32), low],
        )
        rows_in = over_cell(products)
        if step + 1 < ITERS:
            send, u, alpha = call(
                functools.partial(adjoint_send, slots),
                [shape(half + 128), shape(rows), shape(128)], [SMEM] + [VMEM] * 7,
                (lists, *rows_in, u, beta, tiles), adjoint_scratch,
            )
            keep, = call(
                functools.partial(adjoint_keep, slots), [shape(half + 128)],
                [SMEM] + [VMEM] * 2, (lists, u, tiles), adjoint_scratch,
            )
        else:
            squares, alpha = call(
                last_norm, [shape(128), shape(128)], [VMEM] * 6, (*rows_in, u, beta)
            )
        alphas.append(alpha)
    so_far = call(
        gather_up, [shape(half)] * 4 + [shape(128)] * 2, [VMEM] * (4 * ITERS),
        (*owns, *others, *alphas, *betas),
    )
    x, misfit = call(
        finish, [shape(2 * half), jax.ShapeDtypeStruct((1, nrhs), F32)], [VMEM] * 10,
        (*spread(squares + swap(squares), "z"), *so_far),
    )
    return x, misfit.reshape(nrhs)


def solution(mesh):
    parts = Mesh(mesh.devices.reshape(4, 2, 4, 4), ("z", "core", "x", "y"))
    ray, cell = ("z", "core"), ("x", "y")
    in_specs = (P(None, ray), P(ray, cell, None, None), P(ray, cell), P(ray, cell))
    out_specs = (P(None, cell), P())
    return jax.shard_map(local, mesh=parts, in_specs=in_specs, out_specs=out_specs, check_vma=False)
```

```python
import functools

import jax
import jax.numpy as jnp
from jax import lax
from jax.experimental import pallas as pl
from jax.experimental.pallas import tpu as pltpu
from jax.sharding import Mesh, PartitionSpec as P

BLK_DEV = 32
HEAD = 20
GROUP = 4
ITERS = 4
EPS = 1e-06
TINY = 1e-30
DIGITS = 8192.0
CODES = 32000.0
F32 = jnp.float32
BF16 = jnp.bfloat16

VMEM = pl.BlockSpec(memory_space=pltpu.VMEM)
SMEM = pl.BlockSpec(memory_space=pltpu.SMEM)
HBM = pl.BlockSpec(memory_space=pltpu.HBM)


def lane_sum(x):
    return jnp.sum(x, axis=1, keepdims=True)


def fold_sq(x, width):
    total = None
    for at in range(0, x.shape[1], width):
        piece = x[:, at : at + width]
        total = piece * piece if total is None else total + piece * piece
    return total


def two_parts(x):
    return jnp.concatenate([x, x - x.astype(BF16).astype(F32)], axis=0).astype(BF16)


def product(rows, tile):
    both = jnp.dot(rows, tile, preferred_element_type=F32)
    half = both.shape[0] // 2
    return both[:half] + both[half:]


def wide(x):
    return jnp.broadcast_to(x, (x.shape[0], 128))


def slots_of(pattern_ref, counts_ref, second, dead):
    blocks = BLK_DEV // 2
    core = lax.axis_index("core")

    def block_of(b, s):
        found = pattern_ref[s, b]
        within = found % blocks
        at = jnp.where(found // blocks == core, within, within + second)
        return jnp.where(s < counts_ref[0, b], at, dead)

    return block_of


def fill_lists(pattern_ref, counts_ref, lists_ref):
    slots, bundles = pattern_ref.shape
    most = slots * bundles
    blocks = BLK_DEV // 2
    core = lax.axis_index("core")
    for i in range(most):
        for at, value in ((0, 0), (most, blocks), (2 * most, 0), (3 * most, blocks)):
            lists_ref[at + i] = jnp.int32(value)
    lengths = [jnp.int32(0), jnp.int32(0)]
    for b in range(bundles):
        for s in range(slots):
            found = pattern_ref[s, b]
            mine = (found // blocks == core).astype(jnp.int32)
            live = (s < counts_ref[0, b]).astype(jnp.int32)
            at = jnp.where(mine == 1, 2 * most + lengths[1], lengths[0])
            at = jnp.where(live == 1, at, 4 * most + 2)
            lists_ref[at] = jnp.int32(b * slots + s)
            lists_ref[at + most] = found % blocks
            lengths = [lengths[0] + live * (1 - mine), lengths[1] + live * mine]
    lists_ref[4 * most] = lengths[0]
    lists_ref[4 * most + 1] = lengths[1]


def listed_products(lists_ref, mine, tiles_ref, one):
    most = tiles_ref.shape[0]
    base = 2 * most if mine else 0

    def run(first, count):
        for i in range(count):
            one(lists_ref[first + i], lists_ref[first + i + most])

    def group(g, carry):
        run(base + HEAD + g * GROUP, GROUP)
        return carry

    run(base, min(HEAD, most))
    if HEAD < most:
        rest = jnp.maximum(lists_ref[4 * most + (1 if mine else 0)] - HEAD, 0)
        lax.fori_loop(0, (rest + GROUP - 1) // GROUP, group, 0)


def half_adjoint(lists_ref, mine, u, tiles_ref, out_ref, acc_ref, low_ref, slots):
    cells = tiles_ref.shape[2]
    rays = tiles_ref.shape[1]
    half = out_ref.shape[1] - 128
    acc_ref[...] = jnp.zeros_like(acc_ref)
    low_ref[...] = two_parts(u)

    def one(tile, block):
        rows = low_ref[:, pl.ds(pl.multiple_of(tile // slots * rays, rays), rays)]
        part = product(rows, tiles_ref[tile])
        acc_ref[:, pl.ds(pl.multiple_of(block * cells, cells), cells)] += part

    listed_products(lists_ref, mine, tiles_ref, one)
    out_ref[:, :half] = acc_ref[:, :half]
    out_ref[:, half:] = fold_sq(u, 128)


def half_forward(lists_ref, mine, v, tiles_ref, sum_ref, low_ref, slots):
    cells, rays = tiles_ref.shape[1:]
    half = v.shape[1]
    low_ref[:, :half] = two_parts(v)
    low_ref[:, half:] = jnp.zeros((low_ref.shape[0], cells), BF16)

    def one(tile, block):
        rows = low_ref[:, pl.ds(pl.multiple_of(block * cells, cells), cells)]
        part = product(rows, tiles_ref[tile])
        sum_ref[:, pl.ds(pl.multiple_of(tile // slots * rays, rays), rays)] += part

    listed_products(lists_ref, mine, tiles_ref, one)


def scatter_products(u, block_of, tiles_ref, keep_ref, send_ref, acc_ref, copies=None):
    bundles, slots, rays, cells = tiles_ref.shape
    half = keep_ref.shape[1] - 128
    acc_ref[...] = jnp.zeros_like(acc_ref)
    low = two_parts(u)
    for b in range(bundles):
        if copies:
            copies[b].wait()
        rows = low[:, b * rays : (b + 1) * rays]
        for s in range(slots):
            part = product(rows, tiles_ref[b, s])
            at = pl.multiple_of(block_of(b, s) * cells, cells)
            acc_ref[:, pl.ds(at, cells)] += part
    squares = fold_sq(u, 128)
    for out_ref, at in ((keep_ref, 0), (send_ref, half + cells)):
        out_ref[:, :half] = acc_ref[:, at : at + half]
        out_ref[:, half:] = squares


def first_adjoint(
    source_p_ref, source_c_ref, source_u_ref, source_ref, keep_ref, send_ref, tiles_ref, acc_ref,
    pattern_ref, counts_ref, u_ref, sem,
):
    bundles = source_ref.shape[0]
    small = ((source_p_ref, pattern_ref), (source_c_ref, counts_ref), (source_u_ref, u_ref))
    first = [
        pltpu.make_async_copy(source, target, sem.at[bundles + at])
        for at, (source, target) in enumerate(small)
    ]
    copies = [
        pltpu.make_async_copy(source_ref.at[b], tiles_ref.at[b], sem.at[b])
        for b in range(bundles)
    ]
    for copy in first + copies:
        copy.start()
    for copy in first:
        copy.wait()
    put = slots_of(pattern_ref, counts_ref, BLK_DEV // 2 + 1, BLK_DEV // 2)
    scatter_products(u_ref[...], put, tiles_ref, keep_ref, send_ref, acc_ref, copies)


def split(value, digits):
    power = jnp.floor(jnp.log2(value))
    return power, value * jnp.exp2(-power) * digits


def encode(body, squares, out_ref):
    width = body.shape[1]
    peak = jnp.maximum(jnp.max(jnp.abs(body), axis=1, keepdims=True), TINY)
    power, mantissa = split(peak, DIGITS)
    mantissa = jnp.floor(mantissa) + 1.0
    scale = mantissa * jnp.exp2(power) * (1.0 / DIGITS)
    norm_power, norm = split(jnp.maximum(squares, TINY), DIGITS)
    high = jnp.floor(norm)
    low = (norm - high) * DIGITS
    lane = lax.broadcasted_iota(jnp.int32, (body.shape[0], 128), 1)
    fields = jnp.zeros_like(lane).astype(F32)
    for at, field in enumerate((power, mantissa, norm_power, high, low)):
        fields = jnp.where(lane == at, field, fields)

    def code(x):
        return jnp.round(x).astype(jnp.int32).astype(jnp.int16)

    out_ref[:, :width] = code(body * (CODES / scale))
    out_ref[:, width:] = code(fields)


def decode(ref):
    width = ref.shape[1] - 128
    codes = ref[...].astype(jnp.int32).astype(F32)
    power, mantissa, norm_power, high, low = [codes[:, width + at : width + at + 1] for at in range(5)]
    scale = mantissa * jnp.exp2(power) * (1.0 / DIGITS)
    norm = (high + low * (1.0 / DIGITS)) * jnp.exp2(norm_power) * (1.0 / DIGITS)
    return codes[:, :width] * (scale * (1.0 / CODES)), norm


def decoded_sum(*refs):
    own, left, right, far = [decode(ref) for ref in refs]
    return [(own[at] + far[at]) + (left[at] + right[at]) for at in range(2)]


def pack(keep_ref, other_ref, out_ref):
    total = keep_ref[...] + other_ref[...]
    width = total.shape[1] - 128
    encode(total[:, :width], lane_sum(total[:, width:]), out_ref)


def relay(own_ref, left_ref, right_ref, far_ref, out_ref):
    body, squares = decoded_sum(own_ref, left_ref, right_ref, far_ref)
    encode(body, squares, out_ref)


def ray_vector(own_ref, left_ref, right_ref, far_ref, prev_ref, beta_ref):
    total, squares = decoded_sum(own_ref, left_ref, right_ref, far_ref)
    alpha = jnp.sqrt(squares + EPS)
    u = total / alpha - (alpha / beta_ref[:, :1]) * prev_ref[...]
    return u, alpha


def adjoint_send(
    slots, lists_ref, own_ref, left_ref, right_ref, far_ref, prev_ref, beta_ref, tiles_ref,
    send_ref, u_ref, alpha_ref, acc_ref, low_ref,
):
    u, alpha = ray_vector(own_ref, left_ref, right_ref, far_ref, prev_ref, beta_ref)
    u_ref[...] = u
    alpha_ref[...] = wide(alpha)
    half_adjoint(lists_ref, False, u, tiles_ref, send_ref, acc_ref, low_ref, slots)


def adjoint_keep(slots, lists_ref, u_ref, tiles_ref, keep_ref, acc_ref, low_ref):
    half_adjoint(lists_ref, True, u_ref[...], tiles_ref, keep_ref, acc_ref, low_ref, slots)


def last_norm(
    own_ref, left_ref, right_ref, far_ref, prev_ref, beta_ref, out_ref, alpha_ref
):
    u, alpha = ray_vector(own_ref, left_ref, right_ref, far_ref, prev_ref, beta_ref)
    alpha_ref[...] = wide(alpha)
    out_ref[...] = fold_sq(u, 128)


def cell_vector(
    first, own_ref, left_ref, right_ref, far_ref, prev_ref, alpha_ref, v_ref, beta_ref
):
    total, squares = decoded_sum(own_ref, left_ref, right_ref, far_ref)
    beta = jnp.sqrt(squares + EPS)
    v = total / beta
    if not first:
        v = v - (beta / alpha_ref[:, :1]) * prev_ref[...]
    v_ref[...] = v
    beta_ref[...] = wide(beta)


def turn(pattern_ref, counts_ref, tiles_ref, out_ref, lists_ref):
    fill_lists(pattern_ref, counts_ref, lists_ref)
    for tile in range(tiles_ref.shape[0]):
        out_ref[tile] = tiles_ref[tile].T


def forward_own(slots, lists_ref, own_ref, tiles_ref, part_ref, low_ref):
    part_ref[...] = jnp.zeros_like(part_ref)
    own = own_ref[...]
    half_forward(lists_ref, True, own, tiles_ref, part_ref, low_ref, slots)
    part_ref[:, part_ref.shape[1] - 128 :] = fold_sq(own, 128)


def forward_other(slots, lists_ref, part_ref, other_ref, tiles_ref, out_ref, sum_ref, low_ref):
    width = sum_ref.shape[1]
    sum_ref[...] = part_ref[:, :width]
    other = other_ref[...]
    half_forward(lists_ref, False, other, tiles_ref, sum_ref, low_ref, slots)
    encode(sum_ref[...], lane_sum(part_ref[:, width:] + fold_sq(other, 128)), out_ref)


def gather_up(*refs):
    count = ITERS
    own_refs, other_refs = refs[:count], refs[count : 2 * count]
    alpha_refs, beta_refs = refs[2 * count : 3 * count], refs[3 * count : 4 * count]
    x_refs, w_refs, phibar_ref, rhobar_ref = refs[4 * count : 4 * count + 2], refs[
        4 * count + 2 : 4 * count + 4], refs[-2], refs[-1]
    alphas = [ref[:, :1] for ref in alpha_refs]
    betas = [ref[:, :1] for ref in beta_refs]
    phibar, rhobar = betas[0], alphas[0]
    steps, turns = [], []
    for k in range(count - 1):
        beta = betas[k + 1]
        rho = jnp.sqrt(rhobar * rhobar + beta * beta)
        cosine, sine = rhobar / rho, beta / rho
        steps.append(cosine * phibar / rho)
        phibar = sine * phibar
        turns.append(sine * alphas[k + 1] / rho)
        rhobar = -cosine * alphas[k + 1]
    for refs, x_ref, w_ref in zip((own_refs, other_refs), x_refs, w_refs):
        w = refs[0][...] / alphas[0]
        x = steps[0] * w
        for k in range(1, count):
            w = refs[k][...] / alphas[k] - turns[k - 1] * w
            if k + 1 < count:
                x = x + steps[k] * w
        x_ref[...] = x
        w_ref[...] = w
    phibar_ref[...] = wide(phibar)
    rhobar_ref[...] = wide(rhobar)


def finish(
    own_ref, left_ref, right_ref, far_ref, own_x_ref, other_x_ref, own_w_ref,
    other_w_ref, phibar_ref, rhobar_ref, x_ref, misfit_ref,
):
    width = own_x_ref.shape[1]
    total = (own_ref[...] + far_ref[...]) + (left_ref[...] + right_ref[...])
    beta = jnp.sqrt(lane_sum(total) + EPS)
    phibar, rhobar = phibar_ref[:, :1], rhobar_ref[:, :1]
    rho = jnp.sqrt(rhobar * rhobar + beta * beta)
    step = (rhobar / rho) * phibar / rho
    core = lax.axis_index("core")
    for half, xs_ref, w_ref in ((core, own_x_ref, own_w_ref), (1 - core, other_x_ref, other_w_ref)):
        at = pl.multiple_of(half * width, width)
        x_ref[:, pl.ds(at, width)] = xs_ref[...] + step * w_ref[...]
    last = wide((beta / rho) * phibar)
    row = lax.broadcasted_iota(jnp.int32, last.shape, 0)
    lane = lax.broadcasted_iota(jnp.int32, last.shape, 1)
    across = jnp.sum(jnp.where(row == lane, last, 0.0), axis=0, keepdims=True)
    misfit_ref[...] = across[:, : misfit_ref.shape[1]]


def call(body, outs, specs, args, scratch=(), out_specs=None):
    return pl.pallas_call(
        body,
        out_shape=outs,
        in_specs=specs,
        out_specs=out_specs or [VMEM] * len(outs),
        scratch_shapes=list(scratch),
        compiler_params=pltpu.CompilerParams(vmem_limit_bytes=12 << 20),
    )(*args)


def local(right_side, tiles, pattern, counts):
    nrhs, rows = right_side.shape
    bundles, slots, rays, cells = tiles.shape
    blocks = BLK_DEV // 2
    half = blocks * cells
    most = bundles * slots
    slots_in = (pattern.T, counts.T)

    def shape(columns, dtype=F32):
        return jax.ShapeDtypeStruct((nrhs, columns), dtype)

    def spread(value, axis):
        n = lax.axis_size(axis)
        moved = [
            lax.ppermute(value, axis, [(i, i ^ by) for i in range(n)]) for by in (1, 3, 2)
        ]
        return [value] + moved

    def swap(value):
        return lax.ppermute(value, "core", [(0, 1), (1, 0)])

    def over_cell(partial):
        summed, = call(
            relay, [shape(rows + 128, jnp.int16)], [VMEM] * 4, spread(partial, "x")
        )
        return spread(summed, "y")

    halves = [shape(half + 128)] * 2
    keep, send, tiles = call(
        first_adjoint, halves + [jax.ShapeDtypeStruct(tiles.shape, tiles.dtype)],
        [HBM] * 4,
        [pltpu.with_memory_space_constraint(z, pltpu.HBM) for z in (*slots_in, right_side, tiles)],
        [
            pltpu.VMEM((nrhs, 2 * (half + cells)), F32),
            pltpu.SMEM((slots, bundles), jnp.int32), pltpu.SMEM((1, bundles), jnp.int32),
            pltpu.VMEM(right_side.shape, F32), pltpu.SemaphoreType.DMA((bundles + 3,)),
        ],
    )
    tiles = tiles.reshape(most, rays, cells)
    turned, lists = call(
        turn,
        [
            jax.ShapeDtypeStruct((most, cells, rays), tiles.dtype),
            jax.ShapeDtypeStruct((5 * most + 3,), jnp.int32),
        ],
        [SMEM] * 2 + [VMEM], (*slots_in, tiles), (), [VMEM, SMEM],
    )
    adjoint_scratch = [pltpu.VMEM((nrhs, half + cells), F32), pltpu.VMEM((2 * nrhs, rows), BF16)]
    low = pltpu.VMEM((2 * nrhs, half + cells), BF16)
    u = right_side
    owns, others, alphas, betas = [], [], [], []
    for step in range(ITERS):
        prev = (owns[-1], alphas[-1]) if step else (right_side, right_side)
        packed, = call(
            pack, [shape(half + 128, jnp.int16)], [VMEM] * 2, (keep, swap(send))
        )
        moved = spread(packed, "z")
        if step == 0:
            moved, turned, lists = lax.optimization_barrier((moved, turned, lists))
        v, beta = call(
            functools.partial(cell_vector, step == 0), [shape(half), shape(128)], [VMEM] * 6,
            (*moved, *prev),
        )
        other = swap(v)
        owns.append(v)
        others.append(other)
        betas.append(beta)
        part, = call(
            functools.partial(forward_own, slots), [shape(rows + 128)], [SMEM] + [VMEM] * 2,
            (lists, v, turned), [low],
        )
        products, = call(
            functools.partial(forward_other, slots), [shape(rows + 128, jnp.int16)],
            [SMEM] + [VMEM] * 3, (lists, part, other, turned), [pltpu.VMEM((nrhs, rows), F32), low],
        )
        rows_in = over_cell(products)
        if step + 1 < ITERS:
            send, u, alpha = call(
                functools.partial(adjoint_send, slots),
                [shape(half + 128), shape(rows), shape(128)], [SMEM] + [VMEM] * 7,
                (lists, *rows_in, u, beta, tiles), adjoint_scratch,
            )
            keep, = call(
                functools.partial(adjoint_keep, slots), [shape(half + 128)],
                [SMEM] + [VMEM] * 2, (lists, u, tiles), adjoint_scratch,
            )
        else:
            squares, alpha = call(
                last_norm, [shape(128), shape(128)], [VMEM] * 6, (*rows_in, u, beta)
            )
        alphas.append(alpha)
    so_far = call(
        gather_up, [shape(half)] * 4 + [shape(128)] * 2, [VMEM] * (4 * ITERS),
        (*owns, *others, *alphas, *betas),
    )
    x, misfit = call(
        finish, [shape(2 * half), jax.ShapeDtypeStruct((1, nrhs), F32)], [VMEM] * 10,
        (*spread(squares + swap(squares), "z"), *so_far),
    )
    return x, misfit.reshape(nrhs)


def solution(mesh):
    parts = Mesh(mesh.devices.reshape(4, 2, 4, 4), ("z", "core", "x", "y"))
    ray, cell = ("z", "core"), ("x", "y")
    in_specs = (P(None, ray), P(ray, cell, None, None), P(ray, cell), P(ray, cell))
    out_specs = (P(None, cell), P())
    return jax.shard_map(local, mesh=parts, in_specs=in_specs, out_specs=out_specs, check_vma=False)
```

```python
import functools

import jax
import jax.numpy as jnp
from jax import lax
from jax.experimental import pallas as pl
from jax.experimental.pallas import tpu as pltpu
from jax.sharding import Mesh, PartitionSpec as P

BLK_DEV = 32
HEAD = 18
GROUP = 2
ITERS = 4
EPS = 1e-06
TINY = 1e-30
DIGITS = 8192.0
CODES = 32000.0
F32 = jnp.float32
BF16 = jnp.bfloat16

VMEM = pl.BlockSpec(memory_space=pltpu.VMEM)
SMEM = pl.BlockSpec(memory_space=pltpu.SMEM)
HBM = pl.BlockSpec(memory_space=pltpu.HBM)


def lane_sum(x):
    return jnp.sum(x, axis=1, keepdims=True)


def fold_sq(x, width):
    total = None
    for at in range(0, x.shape[1], width):
        piece = x[:, at : at + width]
        total = piece * piece if total is None else total + piece * piece
    return total


def two_parts(x):
    return jnp.concatenate([x, x - x.astype(BF16).astype(F32)], axis=0).astype(BF16)


def product(rows, tile):
    both = jnp.dot(rows, tile, preferred_element_type=F32)
    half = both.shape[0] // 2
    return both[:half] + both[half:]


def wide(x):
    return jnp.broadcast_to(x, (x.shape[0], 128))


def slots_of(pattern_ref, counts_ref, second, dead):
    blocks = BLK_DEV // 2
    core = lax.axis_index("core")

    def block_of(b, s):
        found = pattern_ref[s, b]
        within = found % blocks
        at = jnp.where(found // blocks == core, within, within + second)
        return jnp.where(s < counts_ref[0, b], at, dead)

    return block_of


def fill_lists(pattern_ref, counts_ref, lists_ref):
    slots, bundles = pattern_ref.shape
    most = slots * bundles
    blocks = BLK_DEV // 2
    core = lax.axis_index("core")
    for i in range(most):
        for at, value in ((0, 0), (most, blocks), (2 * most, 0), (3 * most, blocks)):
            lists_ref[at + i] = jnp.int32(value)
    lengths = [jnp.int32(0), jnp.int32(0)]
    for b in range(bundles):
        for s in range(slots):
            found = pattern_ref[s, b]
            mine = (found // blocks == core).astype(jnp.int32)
            live = (s < counts_ref[0, b]).astype(jnp.int32)
            at = jnp.where(mine == 1, 2 * most + lengths[1], lengths[0])
            at = jnp.where(live == 1, at, 4 * most + 2)
            lists_ref[at] = jnp.int32(b * slots + s)
            lists_ref[at + most] = found % blocks
            lengths = [lengths[0] + live * (1 - mine), lengths[1] + live * mine]
    lists_ref[4 * most] = lengths[0]
    lists_ref[4 * most + 1] = lengths[1]


def listed_products(lists_ref, mine, tiles_ref, one):
    most = tiles_ref.shape[0]
    base = 2 * most if mine else 0

    def run(first, count):
        for i in range(count):
            one(lists_ref[first + i], lists_ref[first + i + most])

    def group(g, carry):
        run(base + HEAD + g * GROUP, GROUP)
        return carry

    run(base, min(HEAD, most))
    if HEAD < most:
        rest = jnp.maximum(lists_ref[4 * most + (1 if mine else 0)] - HEAD, 0)
        lax.fori_loop(0, (rest + GROUP - 1) // GROUP, group, 0)


def half_adjoint(lists_ref, mine, u, tiles_ref, out_ref, acc_ref, low_ref, slots):
    cells = tiles_ref.shape[2]
    rays = tiles_ref.shape[1]
    half = out_ref.shape[1] - 128
    acc_ref[...] = jnp.zeros_like(acc_ref)
    low_ref[...] = two_parts(u)

    def one(tile, block):
        rows = low_ref[:, pl.ds(pl.multiple_of(tile // slots * rays, rays), rays)]
        part = product(rows, tiles_ref[tile])
        acc_ref[:, pl.ds(pl.multiple_of(block * cells, cells), cells)] += part

    listed_products(lists_ref, mine, tiles_ref, one)
    out_ref[:, :half] = acc_ref[:, :half]
    out_ref[:, half:] = fold_sq(u, 128)


def half_forward(lists_ref, mine, v, tiles_ref, sum_ref, low_ref, slots):
    cells, rays = tiles_ref.shape[1:]
    half = v.shape[1]
    low_ref[:, :half] = two_parts(v)
    low_ref[:, half:] = jnp.zeros((low_ref.shape[0], cells), BF16)

    def one(tile, block):
        rows = low_ref[:, pl.ds(pl.multiple_of(block * cells, cells), cells)]
        part = product(rows, tiles_ref[tile])
        sum_ref[:, pl.ds(pl.multiple_of(tile // slots * rays, rays), rays)] += part

    listed_products(lists_ref, mine, tiles_ref, one)


def scatter_products(u, block_of, tiles_ref, keep_ref, send_ref, acc_ref, copies=None):
    bundles, slots, rays, cells = tiles_ref.shape
    half = keep_ref.shape[1] - 128
    acc_ref[...] = jnp.zeros_like(acc_ref)
    low = two_parts(u)
    for b in range(bundles):
        if copies:
            copies[b].wait()
        rows = low[:, b * rays : (b + 1) * rays]
        for s in range(slots):
            part = product(rows, tiles_ref[b, s])
            at = pl.multiple_of(block_of(b, s) * cells, cells)
            acc_ref[:, pl.ds(at, cells)] += part
    squares = fold_sq(u, 128)
    for out_ref, at in ((keep_ref, 0), (send_ref, half + cells)):
        out_ref[:, :half] = acc_ref[:, at : at + half]
        out_ref[:, half:] = squares


def first_adjoint(
    source_p_ref, source_c_ref, source_u_ref, source_ref, keep_ref, send_ref, tiles_ref, acc_ref,
    pattern_ref, counts_ref, u_ref, sem,
):
    bundles = source_ref.shape[0]
    small = ((source_p_ref, pattern_ref), (source_c_ref, counts_ref), (source_u_ref, u_ref))
    first = [
        pltpu.make_async_copy(source, target, sem.at[bundles + at])
        for at, (source, target) in enumerate(small)
    ]
    copies = [
        pltpu.make_async_copy(source_ref.at[b], tiles_ref.at[b], sem.at[b])
        for b in range(bundles)
    ]
    for copy in first + copies:
        copy.start()
    for copy in first:
        copy.wait()
    put = slots_of(pattern_ref, counts_ref, BLK_DEV // 2 + 1, BLK_DEV // 2)
    scatter_products(u_ref[...], put, tiles_ref, keep_ref, send_ref, acc_ref, copies)


def split(value, digits):
    power = jnp.floor(jnp.log2(value))
    return power, value * jnp.exp2(-power) * digits


def encode(body, squares, out_ref):
    width = body.shape[1]
    peak = jnp.maximum(jnp.max(jnp.abs(body), axis=1, keepdims=True), TINY)
    power, mantissa = split(peak, DIGITS)
    mantissa = jnp.floor(mantissa) + 1.0
    scale = mantissa * jnp.exp2(power) * (1.0 / DIGITS)
    norm_power, norm = split(jnp.maximum(squares, TINY), DIGITS)
    high = jnp.floor(norm)
    low = (norm - high) * DIGITS
    lane = lax.broadcasted_iota(jnp.int32, (body.shape[0], 128), 1)
    fields = jnp.zeros_like(lane).astype(F32)
    for at, field in enumerate((power, mantissa, norm_power, high, low)):
        fields = jnp.where(lane == at, field, fields)

    def code(x):
        return jnp.round(x).astype(jnp.int32).astype(jnp.int16)

    out_ref[:, :width] = code(body * (CODES / scale))
    out_ref[:, width:] = code(fields)


def decode(ref):
    width = ref.shape[1] - 128
    codes = ref[...].astype(jnp.int32).astype(F32)
    power, mantissa, norm_power, high, low = [codes[:, width + at : width + at + 1] for at in range(5)]
    scale = mantissa * jnp.exp2(power) * (1.0 / DIGITS)
    norm = (high + low * (1.0 / DIGITS)) * jnp.exp2(norm_power) * (1.0 / DIGITS)
    return codes[:, :width] * (scale * (1.0 / CODES)), norm


def decoded_sum(*refs):
    own, left, right, far = [decode(ref) for ref in refs]
    return [(own[at] + far[at]) + (left[at] + right[at]) for at in range(2)]


def pack(keep_ref, other_ref, out_ref):
    total = keep_ref[...] + other_ref[...]
    width = total.shape[1] - 128
    encode(total[:, :width], lane_sum(total[:, width:]), out_ref)


def relay(own_ref, left_ref, right_ref, far_ref, out_ref):
    body, squares = decoded_sum(own_ref, left_ref, right_ref, far_ref)
    encode(body, squares, out_ref)


def ray_vector(own_ref, left_ref, right_ref, far_ref, prev_ref, beta_ref):
    total, squares = decoded_sum(own_ref, left_ref, right_ref, far_ref)
    alpha = jnp.sqrt(squares + EPS)
    u = total / alpha - (alpha / beta_ref[:, :1]) * prev_ref[...]
    return u, alpha


def adjoint_send(
    slots, lists_ref, own_ref, left_ref, right_ref, far_ref, prev_ref, beta_ref, tiles_ref,
    send_ref, u_ref, alpha_ref, acc_ref, low_ref,
):
    u, alpha = ray_vector(own_ref, left_ref, right_ref, far_ref, prev_ref, beta_ref)
    u_ref[...] = u
    alpha_ref[...] = wide(alpha)
    half_adjoint(lists_ref, False, u, tiles_ref, send_ref, acc_ref, low_ref, slots)


def adjoint_keep(slots, lists_ref, u_ref, tiles_ref, keep_ref, acc_ref, low_ref):
    half_adjoint(lists_ref, True, u_ref[...], tiles_ref, keep_ref, acc_ref, low_ref, slots)


def last_norm(
    own_ref, left_ref, right_ref, far_ref, prev_ref, beta_ref, out_ref, alpha_ref
):
    u, alpha = ray_vector(own_ref, left_ref, right_ref, far_ref, prev_ref, beta_ref)
    alpha_ref[...] = wide(alpha)
    out_ref[...] = fold_sq(u, 128)


def cell_vector(
    first, own_ref, left_ref, right_ref, far_ref, prev_ref, alpha_ref, v_ref, beta_ref
):
    total, squares = decoded_sum(own_ref, left_ref, right_ref, far_ref)
    beta = jnp.sqrt(squares + EPS)
    v = total / beta
    if not first:
        v = v - (beta / alpha_ref[:, :1]) * prev_ref[...]
    v_ref[...] = v
    beta_ref[...] = wide(beta)


def turn(pattern_ref, counts_ref, tiles_ref, out_ref, lists_ref):
    fill_lists(pattern_ref, counts_ref, lists_ref)
    for tile in range(tiles_ref.shape[0]):
        out_ref[tile] = tiles_ref[tile].T


def forward_own(slots, lists_ref, own_ref, tiles_ref, part_ref, low_ref):
    part_ref[...] = jnp.zeros_like(part_ref)
    own = own_ref[...]
    half_forward(lists_ref, True, own, tiles_ref, part_ref, low_ref, slots)
    part_ref[:, part_ref.shape[1] - 128 :] = fold_sq(own, 128)


def forward_other(slots, lists_ref, part_ref, other_ref, tiles_ref, out_ref, sum_ref, low_ref):
    width = sum_ref.shape[1]
    sum_ref[...] = part_ref[:, :width]
    other = other_ref[...]
    half_forward(lists_ref, False, other, tiles_ref, sum_ref, low_ref, slots)
    encode(sum_ref[...], lane_sum(part_ref[:, width:] + fold_sq(other, 128)), out_ref)


def gather_up(*refs):
    count = ITERS
    own_refs, other_refs = refs[:count], refs[count : 2 * count]
    alpha_refs, beta_refs = refs[2 * count : 3 * count], refs[3 * count : 4 * count]
    x_refs, w_refs, phibar_ref, rhobar_ref = refs[4 * count : 4 * count + 2], refs[
        4 * count + 2 : 4 * count + 4], refs[-2], refs[-1]
    alphas = [ref[:, :1] for ref in alpha_refs]
    betas = [ref[:, :1] for ref in beta_refs]
    phibar, rhobar = betas[0], alphas[0]
    steps, turns = [], []
    for k in range(count - 1):
        beta = betas[k + 1]
        rho = jnp.sqrt(rhobar * rhobar + beta * beta)
        cosine, sine = rhobar / rho, beta / rho
        steps.append(cosine * phibar / rho)
        phibar = sine * phibar
        turns.append(sine * alphas[k + 1] / rho)
        rhobar = -cosine * alphas[k + 1]
    for refs, x_ref, w_ref in zip((own_refs, other_refs), x_refs, w_refs):
        w = refs[0][...] / alphas[0]
        x = steps[0] * w
        for k in range(1, count):
            w = refs[k][...] / alphas[k] - turns[k - 1] * w
            if k + 1 < count:
                x = x + steps[k] * w
        x_ref[...] = x
        w_ref[...] = w
    phibar_ref[...] = wide(phibar)
    rhobar_ref[...] = wide(rhobar)


def finish(
    own_ref, left_ref, right_ref, far_ref, own_x_ref, other_x_ref, own_w_ref,
    other_w_ref, phibar_ref, rhobar_ref, x_ref, misfit_ref,
):
    width = own_x_ref.shape[1]
    total = (own_ref[...] + far_ref[...]) + (left_ref[...] + right_ref[...])
    beta = jnp.sqrt(lane_sum(total) + EPS)
    phibar, rhobar = phibar_ref[:, :1], rhobar_ref[:, :1]
    rho = jnp.sqrt(rhobar * rhobar + beta * beta)
    step = (rhobar / rho) * phibar / rho
    core = lax.axis_index("core")
    for half, xs_ref, w_ref in ((core, own_x_ref, own_w_ref), (1 - core, other_x_ref, other_w_ref)):
        at = pl.multiple_of(half * width, width)
        x_ref[:, pl.ds(at, width)] = xs_ref[...] + step * w_ref[...]
    last = wide((beta / rho) * phibar)
    row = lax.broadcasted_iota(jnp.int32, last.shape, 0)
    lane = lax.broadcasted_iota(jnp.int32, last.shape, 1)
    across = jnp.sum(jnp.where(row == lane, last, 0.0), axis=0, keepdims=True)
    misfit_ref[...] = across[:, : misfit_ref.shape[1]]


def call(body, outs, specs, args, scratch=(), out_specs=None):
    return pl.pallas_call(
        body,
        out_shape=outs,
        in_specs=specs,
        out_specs=out_specs or [VMEM] * len(outs),
        scratch_shapes=list(scratch),
        compiler_params=pltpu.CompilerParams(vmem_limit_bytes=12 << 20),
    )(*args)


def local(right_side, tiles, pattern, counts):
    nrhs, rows = right_side.shape
    bundles, slots, rays, cells = tiles.shape
    blocks = BLK_DEV // 2
    half = blocks * cells
    most = bundles * slots
    slots_in = (pattern.T, counts.T)

    def shape(columns, dtype=F32):
        return jax.ShapeDtypeStruct((nrhs, columns), dtype)

    def spread(value, axis):
        n = lax.axis_size(axis)
        moved = [
            lax.ppermute(value, axis, [(i, i ^ by) for i in range(n)]) for by in (1, 3, 2)
        ]
        return [value] + moved

    def swap(value):
        return lax.ppermute(value, "core", [(0, 1), (1, 0)])

    def over_cell(partial):
        summed, = call(
            relay, [shape(rows + 128, jnp.int16)], [VMEM] * 4, spread(partial, "x")
        )
        return spread(summed, "y")

    halves = [shape(half + 128)] * 2
    keep, send, tiles = call(
        first_adjoint, halves + [jax.ShapeDtypeStruct(tiles.shape, tiles.dtype)],
        [HBM] * 4,
        [pltpu.with_memory_space_constraint(z, pltpu.HBM) for z in (*slots_in, right_side, tiles)],
        [
            pltpu.VMEM((nrhs, 2 * (half + cells)), F32),
            pltpu.SMEM((slots, bundles), jnp.int32), pltpu.SMEM((1, bundles), jnp.int32),
            pltpu.VMEM(right_side.shape, F32), pltpu.SemaphoreType.DMA((bundles + 3,)),
        ],
    )
    tiles = tiles.reshape(most, rays, cells)
    turned, lists = call(
        turn,
        [
            jax.ShapeDtypeStruct((most, cells, rays), tiles.dtype),
            jax.ShapeDtypeStruct((5 * most + 3,), jnp.int32),
        ],
        [SMEM] * 2 + [VMEM], (*slots_in, tiles), (), [VMEM, SMEM],
    )
    adjoint_scratch = [pltpu.VMEM((nrhs, half + cells), F32), pltpu.VMEM((2 * nrhs, rows), BF16)]
    low = pltpu.VMEM((2 * nrhs, half + cells), BF16)
    u = right_side
    owns, others, alphas, betas = [], [], [], []
    for step in range(ITERS):
        prev = (owns[-1], alphas[-1]) if step else (right_side, right_side)
        packed, = call(
            pack, [shape(half + 128, jnp.int16)], [VMEM] * 2, (keep, swap(send))
        )
        moved = spread(packed, "z")
        if step == 0:
            moved, turned, lists = lax.optimization_barrier((moved, turned, lists))
        v, beta = call(
            functools.partial(cell_vector, step == 0), [shape(half), shape(128)], [VMEM] * 6,
            (*moved, *prev),
        )
        other = swap(v)
        owns.append(v)
        others.append(other)
        betas.append(beta)
        part, = call(
            functools.partial(forward_own, slots), [shape(rows + 128)], [SMEM] + [VMEM] * 2,
            (lists, v, turned), [low],
        )
        products, = call(
            functools.partial(forward_other, slots), [shape(rows + 128, jnp.int16)],
            [SMEM] + [VMEM] * 3, (lists, part, other, turned), [pltpu.VMEM((nrhs, rows), F32), low],
        )
        rows_in = over_cell(products)
        if step + 1 < ITERS:
            send, u, alpha = call(
                functools.partial(adjoint_send, slots),
                [shape(half + 128), shape(rows), shape(128)], [SMEM] + [VMEM] * 7,
                (lists, *rows_in, u, beta, tiles), adjoint_scratch,
            )
            keep, = call(
                functools.partial(adjoint_keep, slots), [shape(half + 128)],
                [SMEM] + [VMEM] * 2, (lists, u, tiles), adjoint_scratch,
            )
        else:
            squares, alpha = call(
                last_norm, [shape(128), shape(128)], [VMEM] * 6, (*rows_in, u, beta)
            )
        alphas.append(alpha)
    so_far = call(
        gather_up, [shape(half)] * 4 + [shape(128)] * 2, [VMEM] * (4 * ITERS),
        (*owns, *others, *alphas, *betas),
    )
    x, misfit = call(
        finish, [shape(2 * half), jax.ShapeDtypeStruct((1, nrhs), F32)], [VMEM] * 10,
        (*spread(squares + swap(squares), "z"), *so_far),
    )
    return x, misfit.reshape(nrhs)


def solution(mesh):
    parts = Mesh(mesh.devices.reshape(4, 2, 4, 4), ("z", "core", "x", "y"))
    ray, cell = ("z", "core"), ("x", "y")
    in_specs = (P(None, ray), P(ray, cell, None, None), P(ray, cell), P(ray, cell))
    out_specs = (P(None, cell), P())
    return jax.shard_map(local, mesh=parts, in_specs=in_specs, out_specs=out_specs, check_vma=False)
```

```python
import functools

import jax
import jax.numpy as jnp
from jax import lax
from jax.experimental import pallas as pl
from jax.experimental.pallas import tpu as pltpu
from jax.sharding import Mesh, PartitionSpec as P

BLK_DEV = 32
HEAD = 16
GROUP = 4
ITERS = 4
EPS = 1e-06
TINY = 1e-30
DIGITS = 8192.0
CODES = 32000.0
F32 = jnp.float32
BF16 = jnp.bfloat16

VMEM = pl.BlockSpec(memory_space=pltpu.VMEM)
SMEM = pl.BlockSpec(memory_space=pltpu.SMEM)
HBM = pl.BlockSpec(memory_space=pltpu.HBM)


def lane_sum(x):
    return jnp.sum(x, axis=1, keepdims=True)


def fold_sq(x, width):
    total = None
    for at in range(0, x.shape[1], width):
        piece = x[:, at : at + width]
        total = piece * piece if total is None else total + piece * piece
    return total


def two_parts(x):
    return jnp.concatenate([x, x - x.astype(BF16).astype(F32)], axis=0).astype(BF16)


def product(rows, tile):
    both = jnp.dot(rows, tile, preferred_element_type=F32)
    half = both.shape[0] // 2
    return both[:half] + both[half:]


def wide(x):
    return jnp.broadcast_to(x, (x.shape[0], 128))


def slots_of(pattern_ref, counts_ref, second, dead):
    blocks = BLK_DEV // 2
    core = lax.axis_index("core")

    def block_of(b, s):
        found = pattern_ref[s, b]
        within = found % blocks
        at = jnp.where(found // blocks == core, within, within + second)
        return jnp.where(s < counts_ref[0, b], at, dead)

    return block_of


def fill_lists(pattern_ref, counts_ref, lists_ref):
    slots, bundles = pattern_ref.shape
    most = slots * bundles
    blocks = BLK_DEV // 2
    core = lax.axis_index("core")
    for i in range(most):
        for at, value in ((0, 0), (most, blocks), (2 * most, 0), (3 * most, blocks)):
            lists_ref[at + i] = jnp.int32(value)
    lengths = [jnp.int32(0), jnp.int32(0)]
    for b in range(bundles):
        for s in range(slots):
            found = pattern_ref[s, b]
            mine = (found // blocks == core).astype(jnp.int32)
            live = (s < counts_ref[0, b]).astype(jnp.int32)
            at = jnp.where(mine == 1, 2 * most + lengths[1], lengths[0])
            at = jnp.where(live == 1, at, 4 * most + 2)
            lists_ref[at] = jnp.int32(b * slots + s)
            lists_ref[at + most] = found % blocks
            lengths = [lengths[0] + live * (1 - mine), lengths[1] + live * mine]
    lists_ref[4 * most] = lengths[0]
    lists_ref[4 * most + 1] = lengths[1]


def listed_products(lists_ref, mine, tiles_ref, one):
    most = tiles_ref.shape[0]
    base = 2 * most if mine else 0

    def run(first, count):
        for i in range(count):
            one(lists_ref[first + i], lists_ref[first + i + most])

    def group(g, carry):
        run(base + HEAD + g * GROUP, GROUP)
        return carry

    run(base, min(HEAD, most))
    if HEAD < most:
        rest = jnp.maximum(lists_ref[4 * most + (1 if mine else 0)] - HEAD, 0)
        lax.fori_loop(0, (rest + GROUP - 1) // GROUP, group, 0)


def half_adjoint(lists_ref, mine, u, tiles_ref, out_ref, acc_ref, low_ref, slots):
    cells = tiles_ref.shape[2]
    rays = tiles_ref.shape[1]
    half = out_ref.shape[1] - 128
    acc_ref[...] = jnp.zeros_like(acc_ref)
    low_ref[...] = two_parts(u)

    def one(tile, block):
        rows = low_ref[:, pl.ds(pl.multiple_of(tile // slots * rays, rays), rays)]
        part = product(rows, tiles_ref[tile])
        acc_ref[:, pl.ds(pl.multiple_of(block * cells, cells), cells)] += part

    listed_products(lists_ref, mine, tiles_ref, one)
    out_ref[:, :half] = acc_ref[:, :half]
    out_ref[:, half:] = fold_sq(u, 128)


def half_forward(lists_ref, mine, v, tiles_ref, sum_ref, low_ref, slots):
    cells, rays = tiles_ref.shape[1:]
    half = v.shape[1]
    low_ref[:, :half] = two_parts(v)
    low_ref[:, half:] = jnp.zeros((low_ref.shape[0], cells), BF16)

    def one(tile, block):
        rows = low_ref[:, pl.ds(pl.multiple_of(block * cells, cells), cells)]
        part = product(rows, tiles_ref[tile])
        sum_ref[:, pl.ds(pl.multiple_of(tile // slots * rays, rays), rays)] += part

    listed_products(lists_ref, mine, tiles_ref, one)


def scatter_products(u, block_of, tiles_ref, keep_ref, send_ref, acc_ref, copies=None):
    bundles, slots, rays, cells = tiles_ref.shape
    half = keep_ref.shape[1] - 128
    acc_ref[...] = jnp.zeros_like(acc_ref)
    low = two_parts(u)
    for b in range(bundles):
        if copies:
            copies[b].wait()
        rows = low[:, b * rays : (b + 1) * rays]
        for s in range(slots):
            part = product(rows, tiles_ref[b, s])
            at = pl.multiple_of(block_of(b, s) * cells, cells)
            acc_ref[:, pl.ds(at, cells)] += part
    squares = fold_sq(u, 128)
    for out_ref, at in ((keep_ref, 0), (send_ref, half + cells)):
        out_ref[:, :half] = acc_ref[:, at : at + half]
        out_ref[:, half:] = squares


def first_adjoint(
    source_p_ref, source_c_ref, source_u_ref, source_ref, keep_ref, send_ref, tiles_ref, acc_ref,
    pattern_ref, counts_ref, u_ref, sem,
):
    bundles = source_ref.shape[0]
    small = ((source_p_ref, pattern_ref), (source_c_ref, counts_ref), (source_u_ref, u_ref))
    first = [
        pltpu.make_async_copy(source, target, sem.at[bundles + at])
        for at, (source, target) in enumerate(small)
    ]
    copies = [
        pltpu.make_async_copy(source_ref.at[b], tiles_ref.at[b], sem.at[b])
        for b in range(bundles)
    ]
    for copy in first + copies:
        copy.start()
    for copy in first:
        copy.wait()
    put = slots_of(pattern_ref, counts_ref, BLK_DEV // 2 + 1, BLK_DEV // 2)
    scatter_products(u_ref[...], put, tiles_ref, keep_ref, send_ref, acc_ref, copies)


def split(value, digits):
    power = jnp.floor(jnp.log2(value))
    return power, value * jnp.exp2(-power) * digits


def encode(body, squares, out_ref):
    width = body.shape[1]
    peak = jnp.maximum(jnp.max(jnp.abs(body), axis=1, keepdims=True), TINY)
    power, mantissa = split(peak, DIGITS)
    mantissa = jnp.floor(mantissa) + 1.0
    scale = mantissa * jnp.exp2(power) * (1.0 / DIGITS)
    norm_power, norm = split(jnp.maximum(squares, TINY), DIGITS)
    high = jnp.floor(norm)
    low = (norm - high) * DIGITS
    lane = lax.broadcasted_iota(jnp.int32, (body.shape[0], 128), 1)
    fields = jnp.zeros_like(lane).astype(F32)
    for at, field in enumerate((power, mantissa, norm_power, high, low)):
        fields = jnp.where(lane == at, field, fields)

    def code(x):
        return jnp.round(x).astype(jnp.int32).astype(jnp.int16)

    out_ref[:, :width] = code(body * (CODES / scale))
    out_ref[:, width:] = code(fields)


def decode(ref):
    width = ref.shape[1] - 128
    codes = ref[...].astype(jnp.int32).astype(F32)
    power, mantissa, norm_power, high, low = [codes[:, width + at : width + at + 1] for at in range(5)]
    scale = mantissa * jnp.exp2(power) * (1.0 / DIGITS)
    norm = (high + low * (1.0 / DIGITS)) * jnp.exp2(norm_power) * (1.0 / DIGITS)
    return codes[:, :width] * (scale * (1.0 / CODES)), norm


def decoded_sum(*refs):
    own, left, right, far = [decode(ref) for ref in refs]
    return [(own[at] + far[at]) + (left[at] + right[at]) for at in range(2)]


def pack(keep_ref, other_ref, out_ref):
    total = keep_ref[...] + other_ref[...]
    width = total.shape[1] - 128
    encode(total[:, :width], lane_sum(total[:, width:]), out_ref)


def relay(own_ref, left_ref, right_ref, far_ref, out_ref):
    body, squares = decoded_sum(own_ref, left_ref, right_ref, far_ref)
    encode(body, squares, out_ref)


def ray_vector(own_ref, left_ref, right_ref, far_ref, prev_ref, beta_ref):
    total, squares = decoded_sum(own_ref, left_ref, right_ref, far_ref)
    alpha = jnp.sqrt(squares + EPS)
    u = total / alpha - (alpha / beta_ref[:, :1]) * prev_ref[...]
    return u, alpha


def adjoint_send(
    slots, lists_ref, own_ref, left_ref, right_ref, far_ref, prev_ref, beta_ref, tiles_ref,
    send_ref, u_ref, alpha_ref, acc_ref, low_ref,
):
    u, alpha = ray_vector(own_ref, left_ref, right_ref, far_ref, prev_ref, beta_ref)
    u_ref[...] = u
    alpha_ref[...] = wide(alpha)
    half_adjoint(lists_ref, False, u, tiles_ref, send_ref, acc_ref, low_ref, slots)


def adjoint_keep(slots, lists_ref, u_ref, tiles_ref, keep_ref, acc_ref, low_ref):
    half_adjoint(lists_ref, True, u_ref[...], tiles_ref, keep_ref, acc_ref, low_ref, slots)


def last_norm(
    own_ref, left_ref, right_ref, far_ref, prev_ref, beta_ref, out_ref, alpha_ref
):
    u, alpha = ray_vector(own_ref, left_ref, right_ref, far_ref, prev_ref, beta_ref)
    alpha_ref[...] = wide(alpha)
    out_ref[...] = fold_sq(u, 128)


def cell_vector(
    first, own_ref, left_ref, right_ref, far_ref, prev_ref, alpha_ref, v_ref, beta_ref
):
    total, squares = decoded_sum(own_ref, left_ref, right_ref, far_ref)
    beta = jnp.sqrt(squares + EPS)
    v = total / beta
    if not first:
        v = v - (beta / alpha_ref[:, :1]) * prev_ref[...]
    v_ref[...] = v
    beta_ref[...] = wide(beta)


def turn(pattern_ref, counts_ref, tiles_ref, out_ref, lists_ref):
    fill_lists(pattern_ref, counts_ref, lists_ref)
    for tile in range(tiles_ref.shape[0]):
        out_ref[tile] = tiles_ref[tile].T


def forward_own(slots, lists_ref, own_ref, tiles_ref, part_ref, low_ref):
    part_ref[...] = jnp.zeros_like(part_ref)
    own = own_ref[...]
    half_forward(lists_ref, True, own, tiles_ref, part_ref, low_ref, slots)
    part_ref[:, part_ref.shape[1] - 128 :] = fold_sq(own, 128)


def forward_other(slots, lists_ref, part_ref, other_ref, tiles_ref, out_ref, sum_ref, low_ref):
    width = sum_ref.shape[1]
    sum_ref[...] = part_ref[:, :width]
    other = other_ref[...]
    half_forward(lists_ref, False, other, tiles_ref, sum_ref, low_ref, slots)
    encode(sum_ref[...], lane_sum(part_ref[:, width:] + fold_sq(other, 128)), out_ref)


def gather_up(*refs):
    count = ITERS
    own_refs, other_refs = refs[:count], refs[count : 2 * count]
    alpha_refs, beta_refs = refs[2 * count : 3 * count], refs[3 * count : 4 * count]
    x_refs, w_refs, phibar_ref, rhobar_ref = refs[4 * count : 4 * count + 2], refs[
        4 * count + 2 : 4 * count + 4], refs[-2], refs[-1]
    alphas = [ref[:, :1] for ref in alpha_refs]
    betas = [ref[:, :1] for ref in beta_refs]
    phibar, rhobar = betas[0], alphas[0]
    steps, turns = [], []
    for k in range(count - 1):
        beta = betas[k + 1]
        rho = jnp.sqrt(rhobar * rhobar + beta * beta)
        cosine, sine = rhobar / rho, beta / rho
        steps.append(cosine * phibar / rho)
        phibar = sine * phibar
        turns.append(sine * alphas[k + 1] / rho)
        rhobar = -cosine * alphas[k + 1]
    for refs, x_ref, w_ref in zip((own_refs, other_refs), x_refs, w_refs):
        w = refs[0][...] / alphas[0]
        x = steps[0] * w
        for k in range(1, count):
            w = refs[k][...] / alphas[k] - turns[k - 1] * w
            if k + 1 < count:
                x = x + steps[k] * w
        x_ref[...] = x
        w_ref[...] = w
    phibar_ref[...] = wide(phibar)
    rhobar_ref[...] = wide(rhobar)


def finish(
    own_ref, left_ref, right_ref, far_ref, own_x_ref, other_x_ref, own_w_ref,
    other_w_ref, phibar_ref, rhobar_ref, x_ref, misfit_ref,
):
    width = own_x_ref.shape[1]
    total = (own_ref[...] + far_ref[...]) + (left_ref[...] + right_ref[...])
    beta = jnp.sqrt(lane_sum(total) + EPS)
    phibar, rhobar = phibar_ref[:, :1], rhobar_ref[:, :1]
    rho = jnp.sqrt(rhobar * rhobar + beta * beta)
    step = (rhobar / rho) * phibar / rho
    core = lax.axis_index("core")
    for half, xs_ref, w_ref in ((core, own_x_ref, own_w_ref), (1 - core, other_x_ref, other_w_ref)):
        at = pl.multiple_of(half * width, width)
        x_ref[:, pl.ds(at, width)] = xs_ref[...] + step * w_ref[...]
    last = wide((beta / rho) * phibar)
    row = lax.broadcasted_iota(jnp.int32, last.shape, 0)
    lane = lax.broadcasted_iota(jnp.int32, last.shape, 1)
    across = jnp.sum(jnp.where(row == lane, last, 0.0), axis=0, keepdims=True)
    misfit_ref[...] = across[:, : misfit_ref.shape[1]]


def call(body, outs, specs, args, scratch=(), out_specs=None):
    return pl.pallas_call(
        body,
        out_shape=outs,
        in_specs=specs,
        out_specs=out_specs or [VMEM] * len(outs),
        scratch_shapes=list(scratch),
        compiler_params=pltpu.CompilerParams(vmem_limit_bytes=12 << 20),
    )(*args)


def local(right_side, tiles, pattern, counts):
    nrhs, rows = right_side.shape
    bundles, slots, rays, cells = tiles.shape
    blocks = BLK_DEV // 2
    half = blocks * cells
    most = bundles * slots
    slots_in = (pattern.T, counts.T)

    def shape(columns, dtype=F32):
        return jax.ShapeDtypeStruct((nrhs, columns), dtype)

    def spread(value, axis):
        n = lax.axis_size(axis)
        moved = [
            lax.ppermute(value, axis, [(i, i ^ by) for i in range(n)]) for by in (1, 3, 2)
        ]
        return [value] + moved

    def swap(value):
        return lax.ppermute(value, "core", [(0, 1), (1, 0)])

    def over_cell(partial):
        summed, = call(
            relay, [shape(rows + 128, jnp.int16)], [VMEM] * 4, spread(partial, "x")
        )
        return spread(summed, "y")

    halves = [shape(half + 128)] * 2
    keep, send, tiles = call(
        first_adjoint, halves + [jax.ShapeDtypeStruct(tiles.shape, tiles.dtype)],
        [HBM] * 4,
        [pltpu.with_memory_space_constraint(z, pltpu.HBM) for z in (*slots_in, right_side, tiles)],
        [
            pltpu.VMEM((nrhs, 2 * (half + cells)), F32),
            pltpu.SMEM((slots, bundles), jnp.int32), pltpu.SMEM((1, bundles), jnp.int32),
            pltpu.VMEM(right_side.shape, F32), pltpu.SemaphoreType.DMA((bundles + 3,)),
        ],
    )
    tiles = tiles.reshape(most, rays, cells)
    turned, lists = call(
        turn,
        [
            jax.ShapeDtypeStruct((most, cells, rays), tiles.dtype),
            jax.ShapeDtypeStruct((5 * most + 3,), jnp.int32),
        ],
        [SMEM] * 2 + [VMEM], (*slots_in, tiles), (), [VMEM, SMEM],
    )
    adjoint_scratch = [pltpu.VMEM((nrhs, half + cells), F32), pltpu.VMEM((2 * nrhs, rows), BF16)]
    low = pltpu.VMEM((2 * nrhs, half + cells), BF16)
    u = right_side
    owns, others, alphas, betas = [], [], [], []
    for step in range(ITERS):
        prev = (owns[-1], alphas[-1]) if step else (right_side, right_side)
        packed, = call(
            pack, [shape(half + 128, jnp.int16)], [VMEM] * 2, (keep, swap(send))
        )
        moved = spread(packed, "z")
        if step == 0:
            moved, turned, lists = lax.optimization_barrier((moved, turned, lists))
        v, beta = call(
            functools.partial(cell_vector, step == 0), [shape(half), shape(128)], [VMEM] * 6,
            (*moved, *prev),
        )
        other = swap(v)
        owns.append(v)
        others.append(other)
        betas.append(beta)
        part, = call(
            functools.partial(forward_own, slots), [shape(rows + 128)], [SMEM] + [VMEM] * 2,
            (lists, v, turned), [low],
        )
        products, = call(
            functools.partial(forward_other, slots), [shape(rows + 128, jnp.int16)],
            [SMEM] + [VMEM] * 3, (lists, part, other, turned), [pltpu.VMEM((nrhs, rows), F32), low],
        )
        rows_in = over_cell(products)
        if step + 1 < ITERS:
            send, u, alpha = call(
                functools.partial(adjoint_send, slots),
                [shape(half + 128), shape(rows), shape(128)], [SMEM] + [VMEM] * 7,
                (lists, *rows_in, u, beta, tiles), adjoint_scratch,
            )
            keep, = call(
                functools.partial(adjoint_keep, slots), [shape(half + 128)],
                [SMEM] + [VMEM] * 2, (lists, u, tiles), adjoint_scratch,
            )
        else:
            squares, alpha = call(
                last_norm, [shape(128), shape(128)], [VMEM] * 6, (*rows_in, u, beta)
            )
        alphas.append(alpha)
    so_far = call(
        gather_up, [shape(half)] * 4 + [shape(128)] * 2, [VMEM] * (4 * ITERS),
        (*owns, *others, *alphas, *betas),
    )
    x, misfit = call(
        finish, [shape(2 * half), jax.ShapeDtypeStruct((1, nrhs), F32)], [VMEM] * 10,
        (*spread(squares + swap(squares), "z"), *so_far),
    )
    return x, misfit.reshape(nrhs)


def solution(mesh):
    parts = Mesh(mesh.devices.reshape(4, 2, 4, 4), ("z", "core", "x", "y"))
    ray, cell = ("z", "core"), ("x", "y")
    in_specs = (P(None, ray), P(ray, cell, None, None), P(ray, cell), P(ray, cell))
    out_specs = (P(None, cell), P())
    return jax.shard_map(local, mesh=parts, in_specs=in_specs, out_specs=out_specs, check_vma=False)
```
